256 devices in a mesh: expert: 4 (over z_lo), dp: 64 (over y, x, z_hi, core).
Axes of the slice: x: 4, y: 4, z: 8 (z_hi: 2, z_lo: 4; z = z_hi * 4 + z_lo), core: 2. Of those that a mesh axis runs over, the one named last changes fastest.
Arguments:
- act_attn: bfloat16 [65536, 256], P(('expert', 'dp')), may hold values from -10 to 10
- dy_attn: bfloat16 [65536, 6144], P(('expert', 'dp')), may hold values from -10 to 10
- act_exp: bfloat16 [4, 8192, 128], P('expert', 'dp'), may hold values from -10 to 10
- dy_exp: bfloat16 [4, 8192, 6144], P('expert', 'dp'), may hold values from -10 to 10
- w_attn: float32 [256, 6144], P(('expert', 'dp')), may hold values from -0.3 to 0.3
- m_attn: float32 [256, 6144], P(('expert', 'dp')), may hold values from -1.5 to 1.5
- v_attn: float32 [256, 6144], P(('expert', 'dp')), may hold values from 0.05 to 1
- w_exp: float32 [4, 128, 6144], P('expert', 'dp'), may hold values from -0.3 to 0.3
- m_exp: float32 [4, 128, 6144], P('expert', 'dp'), may hold values from -1.5 to 1.5
- v_exp: float32 [4, 128, 6144], P('expert', 'dp'), may hold values from 0.05 to 1
Outputs:
- w_attn_new: float32 [256, 6144], P(('expert', 'dp'))
- m_attn_new: float32 [256, 6144], P(('expert', 'dp'))
- v_attn_new: float32 [256, 6144], P(('expert', 'dp'))
- w_exp_new: float32 [4, 128, 6144], P('expert', 'dp')
- m_exp_new: float32 [4, 128, 6144], P('expert', 'dp')
- v_exp_new: float32 [4, 128, 6144], P('expert', 'dp')
- attn_weights: bfloat16 [256, 6144], replicated
- expert_weights: bfloat16 [4, 128, 6144], P('expert')
The draws below stay inside these ranges and needn't reach their ends.
All inputs are finite; a program needn't handle non-finite values.
Results may differ from the reference program's by a relative error of at most 0.0075.
Values may be sent and summed in bfloat16 or wider, within the bound.
A program may use at most 64 MiB of HBM per device.

```python
import math
import jax
import jax.numpy as jnp
from jax import lax

D = 6144
TOK_DEV = 256
EXP_TOK_DEV = 128
ATT_ROWS = 256
EXP_ROWS = 128
TOKENS = 65536
EXP_TOKENS = 8192
PARAMS = 4718592
N_EXPERT = 4


def rows_draw(key, lead, count, rows):
    shape = lead + (count, rows)
    levels = 0.25 * jnp.exp(math.log(10.0) * jnp.arange(rows, dtype=jnp.float32) / max(rows - 1, 1))
    base = jax.random.normal(key, shape, jnp.float32)
    return (jnp.clip(base, -4.0, 4.0) * levels).astype(jnp.bfloat16)


def cols_draw(key, lead, count, cols, block):
    shape = lead + (count, cols)
    order = jax.random.permutation(jax.random.fold_in(key, 5), cols).astype(jnp.float32)
    levels = 0.25 * jnp.exp(math.log(10.0) * order / max(cols - 1, 1))
    blocks = count // block
    block_log = jax.random.uniform(jax.random.fold_in(key, 7), lead + (blocks, 1, 1), jnp.float32, math.log(0.25), 0.0)
    block_scale = jnp.exp(block_log)
    base = jax.random.normal(key, shape, jnp.float32)
    values = jnp.clip(base, -4.0, 4.0) * levels
    values = values.reshape(lead + (blocks, block, cols)) * block_scale
    return values.reshape(shape).astype(jnp.bfloat16)


def draw_act_attn(key, part):
    return rows_draw(jax.random.fold_in(key, 101), (), TOKENS, ATT_ROWS)


def draw_dy_attn(key, part):
    return cols_draw(jax.random.fold_in(key, 202), (), TOKENS, D, TOK_DEV)


def draw_act_exp(key, part):
    return rows_draw(jax.random.fold_in(key, 303), (N_EXPERT,), EXP_TOKENS, EXP_ROWS)


def draw_dy_exp(key, part):
    return cols_draw(jax.random.fold_in(key, 404), (N_EXPERT,), EXP_TOKENS, D, EXP_TOK_DEV)


def level_of(own_key, extent, split, low, top_value):
    loudness = 1.0
    for dim, parts in split:
        heights = jax.random.uniform(jax.random.fold_in(jax.random.fold_in(own_key, 6), dim), (parts,), jnp.float32, low / len(split), top_value / len(split))
        loudness = loudness * jnp.repeat(jnp.exp(heights), extent[dim] // parts).reshape((-1,) + (1,) * (len(extent) - 1 - dim))
    return loudness


def scatter_about(own_key, shape, deviation, bound, shards=(), kind=jnp.bfloat16):
    level = level_of(own_key, shape, shards, -0.22, 0.18) if shards else 1.0
    result = jax.random.normal(own_key, shape, jnp.float32) * deviation * level
    return jnp.minimum(jnp.maximum(result, -bound), bound).astype(kind)


def setup_inputs(seed: int = 0) -> dict:
    arg_keys = jax.random.split(jax.random.key(seed), 11)
    act_attn = draw_act_attn(jax.random.fold_in(arg_keys[10], 71), 0)
    dy_attn = draw_dy_attn(jax.random.fold_in(arg_keys[10], 71), 0)
    act_exp = draw_act_exp(jax.random.fold_in(arg_keys[10], 71), 0)
    dy_exp = draw_dy_exp(jax.random.fold_in(arg_keys[10], 71), 0)
    w_attn = scatter_about(arg_keys[4], (ATT_ROWS, D), 0.05, 0.3, ((0, 256),), jnp.float32)
    m_attn = scatter_about(arg_keys[5], (ATT_ROWS, D), 0.3, 1.5, ((0, 256),), jnp.float32)
    v_attn = jnp.clip(jnp.exp(math.log(1.0) - 2.9957323 * jax.random.uniform(arg_keys[6], (ATT_ROWS, D), jnp.float32) ** level_of(arg_keys[6], (ATT_ROWS, D), ((0, 256),), -0.2, 0.2)), 0.05, 1.0)
    w_exp = scatter_about(arg_keys[7], (N_EXPERT, EXP_ROWS, D), 0.05, 0.3, ((0, 4), (1, 64)), jnp.float32)
    m_exp = scatter_about(arg_keys[8], (N_EXPERT, EXP_ROWS, D), 0.3, 1.5, ((0, 4), (1, 64)), jnp.float32)
    v_exp = jnp.clip(jnp.exp(math.log(1.0) - 2.9957323 * jax.random.uniform(arg_keys[9], (N_EXPERT, EXP_ROWS, D), jnp.float32) ** level_of(arg_keys[9], (N_EXPERT, EXP_ROWS, D), ((0, 4), (1, 64)), -0.2, 0.2)), 0.05, 1.0)
    return dict(act_attn=act_attn, dy_attn=dy_attn, act_exp=act_exp, dy_exp=dy_exp, w_attn=w_attn, m_attn=m_attn, v_attn=v_attn, w_exp=w_exp, m_exp=m_exp, v_exp=v_exp)


beta_first = 0.9
beta_second = 0.95
bias_first = 1.0 - 0.9 ** 10
bias_second = 1.0 - 0.95 ** 10
learn_rate = 0.01
decay_rate = 0.1
adam_eps = 1e-08

def contract_rows(left, right):
    return lax.dot_general(left, right, (((0,), (0,)), ((), ())), preferred_element_type=jnp.float32)

def adamw(grad, weight, moment, second, factor):
    scaled = factor * grad
    moment_new = beta_first * moment + (1.0 - beta_first) * scaled
    second_new = beta_second * second + (1.0 - beta_second) * scaled * scaled
    update = moment_new / bias_first / (jnp.sqrt(second_new / bias_second) + adam_eps)
    weight_new = weight - learn_rate * (update + decay_rate * weight)
    return (weight_new, moment_new, second_new)

def reference(act_attn, dy_attn, act_exp, dy_exp, w_attn, m_attn, v_attn, w_exp, m_exp, v_exp):
    g_attn = contract_rows(act_attn, dy_attn)
    g_exp = jnp.stack([contract_rows(act_exp[index], dy_exp[index]) for index in range(N_EXPERT)])
    total = jnp.sum(g_attn * g_attn) + jnp.sum(g_exp * g_exp)
    norm = jnp.sqrt(total)
    factor = jnp.minimum(1.0, 0.5 * math.sqrt(PARAMS) / (norm + 1e-06))
    wa_new, ma_new, va_new = adamw(g_attn, w_attn, m_attn, v_attn, factor)
    we_new, me_new, ve_new = adamw(g_exp, w_exp, m_exp, v_exp, factor)
    return (wa_new, ma_new, va_new, we_new, me_new, ve_new, wa_new.astype(jnp.bfloat16), we_new.astype(jnp.bfloat16))
```

```python
import math

import jax
import jax.numpy as jnp
from jax import lax
from jax.experimental import pallas as pl
from jax.experimental.pallas import tpu as pltpu
from jax.sharding import PartitionSpec as P

beta_first = 0.9
beta_second = 0.95
bias_first = 1.0 - 0.9**10
bias_second = 1.0 - 0.95**10
learn_rate = 0.01
decay_rate = 0.1
adam_eps = 1e-08

MESH = pl.DeviceIdType.MESH
F32 = jnp.float32
BF16 = jnp.bfloat16
HALF = 3072
PART = 1536
LANES = 128
ROWS = HALF // LANES
PROWS = PART // LANES
STEP = 512


def adamw(grad, weight, moment, second, factor):
    scaled = factor * grad
    moment_new = beta_first * moment + (1.0 - beta_first) * scaled
    second_new = beta_second * second + (1.0 - beta_second) * scaled * scaled
    update = moment_new / bias_first / (jnp.sqrt(second_new / bias_second) + adam_eps)
    weight_new = weight - learn_rate * (update + decay_rate * weight)
    return (weight_new, moment_new, second_new)


def grouped(row):
    low = row & 3
    x = (row >> 2) & 3
    y = (row >> 4) & 3
    z_lo = row >> 6
    return ((y * 4 + x) * 4 + z_lo) * 4 + low


def device_at(z, y, x, core):
    return (lax.rem(z, 4), ((y * 4 + x) * 2 + lax.div(z, 4)) * 2 + core)


def aligned(index, multiple):
    return pl.multiple_of(index, multiple)


def comm_kernel(
    limit,
    act_a, dy_a, act_e, dy_e, w_a, m_a, v_a, w_e, m_e, v_e,
    g_out, f_out, full_a, full_e,
    lhs_a, lhs_e,
    cs_a, cs_e, cr_a, cr_e,
    own_a, own_e, s1_a, s1_e, r1_a, r1_e,
    own2_a, own2_e, s2_a, s2_e, r2_a, r2_e,
    s3_a, s3_e, r3_a, r3_e,
    n_s, n_r,
    ws_a, ws_e, g3_a, g3_e, gt_a, gt_e,
    send_sem, recv_sem, local_sem,
):
    z_lo = lax.axis_index("expert")
    dp = lax.axis_index("dp")
    core = lax.rem(dp, 2)
    z_hi = lax.rem(lax.div(dp, 2), 2)
    x = lax.rem(lax.div(dp, 4), 4)
    y = lax.div(dp, 16)
    z = z_hi * 4 + z_lo
    other = 1 - core

    def zc_mate(dz, dc):
        oz = lax.rem(z + dz, 8)
        oc = core if dc == 0 else other
        return oz, oc

    def plane_mate(dy, dx):
        return device_at(z, lax.rem(y + dy, 4), lax.rem(x + dx, 4), core)

    barrier = pltpu.get_barrier_semaphore()
    greeted = 0
    for dz in range(8):
        for dc in range(2):
            if dz or dc:
                oz, oc = zc_mate(dz, dc)
                pl.semaphore_signal(barrier, inc=1, device_id=device_at(oz, y, x, oc), device_id_type=MESH)
                greeted += 1
    for dy in range(4):
        for dx in range(4):
            if dy or dx:
                pl.semaphore_signal(barrier, inc=1, device_id=plane_mate(dy, dx), device_id_type=MESH)
                greeted += 1

    sent = []

    def send(src, dst, where):
        i = len(sent)
        copy = pltpu.make_async_remote_copy(
            src_ref=src, dst_ref=dst, send_sem=send_sem.at[i], recv_sem=recv_sem.at[i],
            device_id=where, device_id_type=MESH,
        )
        copy.start()
        sent.append(copy)
        return copy

    kept = []

    def keep(src, dst):
        copy = pltpu.make_async_copy(src, dst, local_sem.at[len(kept)])
        copy.start()
        kept.append(copy)

    r0 = lax.broadcasted_iota(jnp.int32, (256, 256), 0)
    r1 = lax.broadcasted_iota(jnp.int32, (256, 256), 1)
    pick = jnp.where(r0 == grouped(r1), 1.0, 0.0).astype(BF16)
    lhs_a[...] = lax.dot_general(
        pick, act_a[...], (((1,), (1,)), ((), ())), preferred_element_type=F32
    ).astype(BF16)
    e0 = lax.broadcasted_iota(jnp.int32, (128, 128), 0)
    e1 = lax.broadcasted_iota(jnp.int32, (128, 128), 1)
    same = jnp.where(e0 == e1, 1.0, 0.0).astype(BF16)
    lhs_e[...] = lax.dot_general(
        same, act_e[0], (((1,), (1,)), ((), ())), preferred_element_type=F32
    ).astype(BF16)

    def product(lhs, rhs):
        return jnp.dot(lhs, rhs, preferred_element_type=F32)

    copies_c = []
    for part in range(2):
        def other_terms(i, carry):
            at = aligned(i * STEP, STEP)
            col = aligned(other * HALF + part * PART + i * STEP, STEP)
            ga = product(lhs_a[...], dy_a[:, pl.ds(col, STEP)])
            cs_a[part, :, :, pl.ds(at, STEP)] = ga.astype(BF16).reshape(16, 16, STEP)
            ge = product(lhs_e[...], dy_e[0, :, pl.ds(col, STEP)])
            cs_e[part, :, :, pl.ds(at, STEP)] = ge.astype(BF16).reshape(16, 8, STEP)
            return carry

        lax.fori_loop(0, PART // STEP, other_terms, 0)
        if part == 0:
            pl.semaphore_wait(barrier, greeted)
        peer = device_at(z, y, x, other)
        copies_c.append((
            send(cs_a.at[part], cr_a.at[part], peer),
            send(cs_e.at[part], cr_e.at[part], peer),
        ))

    copies_1 = []
    for part in range(2):
        for copy in copies_c[part]:
            copy.wait_recv()

        def own_terms(i, carry):
            at = aligned(i * STEP, STEP)
            col = aligned(core * HALF + part * PART + i * STEP, STEP)
            ga = product(lhs_a[...], dy_a[:, pl.ds(col, STEP)]).reshape(16, 16, STEP)
            ga = ga + cr_a[part, :, :, pl.ds(at, STEP)].astype(F32)
            ga = ga.reshape(4, 4, 16, STEP)
            own_a[part, :, :, :, pl.ds(at, STEP)] = ga
            s1_a[part, :, :, :, pl.ds(at, STEP)] = ga.astype(BF16)
            ge = product(lhs_e[...], dy_e[0, :, pl.ds(col, STEP)]).reshape(16, 8, STEP)
            ge = ge + cr_e[part, :, :, pl.ds(at, STEP)].astype(F32)
            ge = ge.reshape(4, 4, 8, STEP)
            own_e[part, :, :, :, pl.ds(at, STEP)] = ge
            s1_e[part, :, :, :, pl.ds(at, STEP)] = ge.astype(BF16)
            return carry

        lax.fori_loop(0, PART // STEP, own_terms, 0)
        batch = []
        for d in (2, 1, 3):
            for s1, r1 in ((s1_a, r1_a), (s1_e, r1_e)):
                if part == 0:
                    ox = lax.rem(x + d, 4)
                    batch.append(send(s1.at[0, :, ox], r1.at[0, d - 1], plane_mate(0, d)))
                else:
                    oy = lax.rem(y + d, 4)
                    batch.append(send(s1.at[1, oy], r1.at[1, d - 1], plane_mate(d, 0)))
        copies_1.append(batch)

    copies_2 = []
    for part in range(2):
        for copy in copies_1[part]:
            copy.wait_recv()

        def sum_first(b, carry):
            for own, r1, own2, s2 in ((own_a, r1_a, own2_a, s2_a), (own_e, r1_e, own2_e, s2_e)):
                total = own[0, b, x] if part == 0 else own[1, y, b]
                for d in range(3):
                    total = total + r1[part, d, b].astype(F32)
                own2[part, b] = total
                s2[part, b] = total.astype(BF16)
            return carry

        lax.fori_loop(0, 4, sum_first, 0)
        batch = []
        for d in (2, 1, 3):
            for s2, r2 in ((s2_a, r2_a), (s2_e, r2_e)):
                if part == 0:
                    oy = lax.rem(y + d, 4)
                    batch.append(send(s2.at[0, oy], r2.at[0, d - 1], plane_mate(d, 0)))
                else:
                    ox = lax.rem(x + d, 4)
                    batch.append(send(s2.at[1, ox], r2.at[1, d - 1], plane_mate(0, d)))
        copies_2.append(batch)

    for part in range(2):
        for copy in copies_2[part]:
            copy.wait_recv()
        mine = y if part == 0 else x
        for own2, r2, s3, rows in ((own2_a, r2_a, s3_a, 16), (own2_e, r2_e, s3_e, 8)):
            total = own2[part, mine]
            for d in range(3):
                total = total + r2[part, d].astype(F32)
            for t in range(PROWS):
                s3[pl.ds(part * PROWS + t, rows, stride=ROWS), :] = total[:, t * LANES : (t + 1) * LANES]

    copies_3 = []
    for dz in (4, 3, 5, 2, 6, 1, 7, 0):
        for dc in range(2):
            if dz or dc:
                oz, oc = zc_mate(dz, dc)
                q = lax.rem(oz, 4) * 4 + lax.div(oz, 4) * 2 + oc
                copies_3.append(send(
                    s3_a.at[pl.ds(aligned(q * ROWS, 8), ROWS)], r3_a.at[dc, dz], device_at(oz, y, x, oc)
                ))
            if dz in (0, 4) and (dz or dc):
                q = lax.div(oz, 4) * 2 + oc
                copies_3.append(send(
                    s3_e.at[pl.ds(aligned(q * 2 * ROWS, 8), 2 * ROWS)],
                    r3_e.at[dc, dz // 4],
                    device_at(oz, y, x, oc),
                ))
    for copy in copies_3:
        copy.wait_recv()

    my_q = z_lo * 4 + z_hi * 2 + core
    my_e = z_hi * 2 + core
    near = s3_a[pl.ds(aligned(my_q * ROWS, 8), ROWS), :]
    far = r3_a[1, 0]
    for dz in range(1, 8):
        near = near + r3_a[0, dz]
        far = far + r3_a[1, dz]
    near_at = pl.ds(aligned(core * ROWS, 8), ROWS)
    far_at = pl.ds(aligned(other * ROWS, 8), ROWS)
    g_out[0, near_at, :] = near
    g_out[0, far_at, :] = far
    near_e = s3_e[pl.ds(aligned(my_e * 2 * ROWS, 8), 2 * ROWS), :] + r3_e[0, 1]
    far_e = r3_e[1, 0] + r3_e[1, 1]
    for j in range(2):
        g_out[1 + j, near_at, :] = near_e[j * ROWS : (j + 1) * ROWS]
        g_out[1 + j, far_at, :] = far_e[j * ROWS : (j + 1) * ROWS]

    square = jnp.zeros((8, LANES), F32)
    for piece in (near, far, near_e, far_e):
        for i in range(piece.shape[0] // 8):
            block = piece[i * 8 : (i + 1) * 8]
            square = square + block * block
    n_s[0] = square
    batch = []
    for dz in (4, 3, 5, 2, 6, 1, 7, 0):
        for dc in range(2):
            if dz or dc:
                oz, oc = zc_mate(dz, dc)
                batch.append(send(n_s.at[0], n_r.at[0, dz * 2 + dc], device_at(oz, y, x, oc)))
    for copy in batch:
        copy.wait_recv()
    for i in range(1, 16):
        square = square + n_r[0, i]
    n_s[1] = square
    batch = []
    for dy in (2, 1, 3, 0):
        for dx in (2, 1, 3, 0):
            if dy or dx:
                batch.append(send(n_s.at[1], n_r.at[1, dy * 4 + dx], plane_mate(dy, dx)))
    for copy in batch:
        copy.wait_recv()
    for i in range(1, 16):
        square = square + n_r[1, i]
    norm = jnp.sqrt(jnp.sum(square, keepdims=True))
    factor = jnp.minimum(1.0, limit / (norm + 1e-06))
    f_out[...] = jnp.broadcast_to(factor, (8, LANES))

    weight_a = adamw(g_out[0], w_a[...], m_a[...], v_a[...], factor)[0]
    for h in range(2):
        ws_a[h] = weight_a[h * ROWS : (h + 1) * ROWS]
    for j in range(2):
        rows = pl.ds(j, 2 * ROWS, stride=2)
        weight_e = adamw(g_out[1 + j], w_e[rows, :], m_e[rows, :], v_e[rows, :], factor)[0]
        for h in range(2):
            ws_e[h, pl.ds(j * ROWS, ROWS), :] = weight_e[h * ROWS : (h + 1) * ROWS]

    at_a = pl.ds(aligned(my_q * ROWS, 8), ROWS)
    at_e = pl.ds(aligned(my_e * 2 * ROWS, 8), 2 * ROWS)
    batch = []
    for dz in (4, 3, 5, 2, 6, 1, 7, 0):
        for dc in range(2):
            if dz or dc:
                oz, oc = zc_mate(dz, dc)
                batch.append(send(ws_a.at[oc], g3_a.at[at_a], device_at(oz, y, x, oc)))
            if dz in (0, 4) and (dz or dc):
                batch.append(send(ws_e.at[oc], g3_e.at[at_e], device_at(oz, y, x, oc)))
    g3_a[at_a, :] = ws_a[core]
    g3_e[at_e, :] = ws_e[core]
    for copy in batch:
        copy.wait_recv()
    for part in range(2):
        for t in range(PROWS):
            lanes = pl.ds(t * LANES, LANES)
            gt_a[part, y, x, :, lanes] = g3_a[pl.ds(part * PROWS + t, 16, stride=ROWS), :].astype(BF16)
            gt_e[part, y, x, :, lanes] = g3_e[pl.ds(part * PROWS + t, 8, stride=ROWS), :].astype(BF16)

    copies_2 = []
    for part in range(2):
        batch = []
        for d in (2, 1, 3):
            for gt in (gt_a, gt_e):
                where = plane_mate(d, 0) if part == 0 else plane_mate(0, d)
                batch.append(send(gt.at[part, y, x], gt.at[part, y, x], where))
        copies_2.append(batch)
    copies_1 = []
    peer = device_at(z, y, x, other)
    landed = []

    def deliver(part, index):
        for gt, full in ((gt_a, full_a), (gt_e, full_e)):
            if part == 0:
                src, dst = gt.at[0, :, index], full.at[core, 0, :, index]
            else:
                src, dst = gt.at[1, index], full.at[core, 1, index]
            landed.append(send(src, dst, peer))
            keep(src, dst)

    for part in range(2):
        for copy in copies_2[part]:
            copy.wait_recv()
        batch = {}
        for d in (2, 1, 3):
            for gt in (gt_a, gt_e):
                if part == 0:
                    copy = send(gt.at[0, :, x], gt.at[0, :, x], plane_mate(0, d))
                else:
                    copy = send(gt.at[1, y], gt.at[1, y], plane_mate(d, 0))
                batch.setdefault(d, []).append(copy)
        copies_1.append(batch)
        deliver(part, x if part == 0 else y)
    for d in (1, 3, 2):
        for part in range(2):
            for copy in copies_1[part][d]:
                copy.wait_recv()
            deliver(part, lax.rem((x if part == 0 else y) + 4 - d, 4))

    for copy in landed:
        copy.wait_recv()
    for copy in kept:
        copy.wait()
    for copy in sent:
        copy.wait_send()


def finish_kernel(
    full_a, full_e, g, f, w_a, m_a, v_a, w_e, m_e, v_e,
    wa_o, ma_o, va_o, we_o, me_o, ve_o, attn_o, exp_o, pick,
):
    @pl.when(pl.program_id(0) == 0)
    def _():
        r0 = lax.broadcasted_iota(jnp.int32, (256, 256), 0)
        r1 = lax.broadcasted_iota(jnp.int32, (256, 256), 1)
        pick[...] = jnp.where(grouped(r0) == r1, 1.0, 0.0).astype(BF16)
        factor = f[0:1, 0:1]
        new = adamw(g[0], w_a[...], m_a[...], v_a[...], factor)
        for ref, value in zip((wa_o, ma_o, va_o), new):
            ref[...] = value
        for j in range(2):
            rows = pl.ds(j, 2 * ROWS, stride=2)
            new = adamw(g[1 + j], w_e[rows, :], m_e[rows, :], v_e[rows, :], factor)
            for ref, value in zip((we_o, me_o, ve_o), new):
                ref[rows, :] = value

    attn_o[...] = jnp.dot(pick[...], full_a[0], preferred_element_type=F32).astype(BF16)
    exp_o[0] = full_e[0]


def body(act_attn, dy_attn, act_exp, dy_exp, w_attn, m_attn, v_attn, w_exp, m_exp, v_exp):
    width = w_attn.shape[1]
    total_params = width * (act_attn.shape[1] + lax.axis_size("expert") * act_exp.shape[2])
    limit = 0.5 * math.sqrt(total_params)
    attn_state = [v.reshape(2 * ROWS, LANES) for v in (w_attn, m_attn, v_attn)]
    exp_state = [
        v.reshape(2, 2 * ROWS, LANES).transpose(1, 0, 2).reshape(4 * ROWS, LANES)
        for v in (w_exp, m_exp, v_exp)
    ]
    vmem = pl.BlockSpec(memory_space=pltpu.VMEM)
    anywhere = pl.BlockSpec(memory_space=pl.ANY)

    def pair(shape, dtype, *lead):
        return [pltpu.VMEM(lead + (16,) + shape, dtype), pltpu.VMEM(lead + (8,) + shape, dtype)]

    n_send = 160
    g, f, full_a, full_e = pl.pallas_call(
        lambda *refs: comm_kernel(limit, *refs),
        out_shape=(
            jax.ShapeDtypeStruct((3, 2 * ROWS, LANES), F32),
            jax.ShapeDtypeStruct((8, LANES), F32),
            jax.ShapeDtypeStruct((2, 2, 4, 4, 16, PART), BF16),
            jax.ShapeDtypeStruct((2, 2, 4, 4, 8, PART), BF16),
        ),
        in_specs=[vmem] * 10,
        out_specs=(vmem, vmem, anywhere, anywhere),
        scratch_shapes=[
            pltpu.VMEM((256, 256), BF16),
            pltpu.VMEM((128, 128), BF16),
            *pair((PART,), BF16, 2, 16),
            *pair((PART,), BF16, 2, 16),
            *pair((PART,), F32, 2, 4, 4),
            *pair((PART,), BF16, 2, 4, 4),
            *pair((PART,), BF16, 2, 3, 4),
            *pair((PART,), F32, 2, 4),
            *pair((PART,), BF16, 2, 4),
            *pair((PART,), BF16, 2, 3),
            pltpu.VMEM((16 * ROWS, LANES), F32),
            pltpu.VMEM((8 * ROWS, LANES), F32),
            pltpu.VMEM((2, 8, ROWS, LANES), F32),
            pltpu.VMEM((2, 2, 2 * ROWS, LANES), F32),
            pltpu.VMEM((2, 8, LANES), F32),
            pltpu.VMEM((2, 16, 8, LANES), F32),
            pltpu.VMEM((2, ROWS, LANES), F32),
            pltpu.VMEM((2, 2 * ROWS, LANES), F32),
            pltpu.VMEM((16 * ROWS, LANES), F32),
            pltpu.VMEM((8 * ROWS, LANES), F32),
            *pair((PART,), BF16, 2, 4, 4),
            pltpu.SemaphoreType.DMA((n_send,)),
            pltpu.SemaphoreType.DMA((n_send,)),
            pltpu.SemaphoreType.DMA((16,)),
        ],
        compiler_params=pltpu.CompilerParams(
            collective_id=0, has_side_effects=True, vmem_limit_bytes=48 * 1024 * 1024
        ),
    )(act_attn, dy_attn, act_exp, dy_exp, *attn_state, *exp_state)

    steps = width // STEP
    per_part = PART // STEP
    whole = lambda shape: pl.BlockSpec(shape, lambda i: (0,) * len(shape))
    a_shape, e_shape = (2 * ROWS, LANES), (4 * ROWS, LANES)
    outs = pl.pallas_call(
        finish_kernel,
        grid=(steps,),
        out_shape=(
            *[jax.ShapeDtypeStruct(a_shape, F32)] * 3,
            *[jax.ShapeDtypeStruct(e_shape, F32)] * 3,
            jax.ShapeDtypeStruct((256, width), BF16),
            jax.ShapeDtypeStruct((1, 128, width), BF16),
        ),
        in_specs=[
            pl.BlockSpec((1, 256, STEP), lambda i: (i // per_part, 0, i % per_part)),
            pl.BlockSpec((1, 128, STEP), lambda i: (i // per_part, 0, i % per_part)),
            whole((3, 2 * ROWS, LANES)),
            whole((8, LANES)),
            *[whole(a_shape)] * 3,
            *[whole(e_shape)] * 3,
        ],
        out_specs=(
            *[whole(a_shape)] * 3,
            *[whole(e_shape)] * 3,
            pl.BlockSpec((256, STEP), lambda i: (0, i)),
            pl.BlockSpec((1, 128, STEP), lambda i: (0, 0, i)),
        ),
        scratch_shapes=[pltpu.VMEM((256, 256), BF16)],
    )(full_a.reshape(4, 256, PART), full_e.reshape(4, 128, PART), g, f, *attn_state, *exp_state)
    attn_new = [v.reshape(1, width) for v in outs[:3]]
    exp_new = [
        v.reshape(2 * ROWS, 2, LANES).transpose(1, 0, 2).reshape(1, 2, width) for v in outs[3:6]
    ]
    return (*attn_new, *exp_new, outs[6], outs[7])


def solution(mesh):
    rows = P(("expert", "dp"), None)
    owned = P("expert", "dp", None)
    return jax.shard_map(
        body,
        mesh=mesh,
        in_specs=(rows, rows, owned, owned, rows, rows, rows, owned, owned, owned),
        out_specs=(rows, rows, rows, owned, owned, owned, P(), P("expert", None, None)),
        check_vma=False,
    )
```

```python
import math

import jax
import jax.numpy as jnp
from jax import lax
from jax.experimental import pallas as pl
from jax.experimental.pallas import tpu as pltpu
from jax.sharding import PartitionSpec as P

beta_first = 0.9
beta_second = 0.95
bias_first = 1.0 - 0.9**10
bias_second = 1.0 - 0.95**10
learn_rate = 0.01
decay_rate = 0.1
adam_eps = 1e-08

MESH = pl.DeviceIdType.MESH
F32 = jnp.float32
BF16 = jnp.bfloat16
HALF = 3072
PART = 1536
LANES = 128
ROWS = HALF // LANES
PROWS = PART // LANES
STEP = 512
WIDE = 768

def adamw(grad, weight, moment, second, factor):
    scaled = factor * grad
    moment_new = beta_first * moment + (1.0 - beta_first) * scaled
    second_new = beta_second * second + (1.0 - beta_second) * scaled * scaled
    update = moment_new / bias_first / (jnp.sqrt(second_new / bias_second) + adam_eps)
    weight_new = weight - learn_rate * (update + decay_rate * weight)
    return (weight_new, moment_new, second_new)

def grouped(row):
    low = row & 3
    x = (row >> 2) & 3
    y = (row >> 4) & 3
    z_lo = row >> 6
    return ((y * 4 + x) * 4 + z_lo) * 4 + low

def device_at(z, y, x, core):
    return (lax.rem(z, 4), ((y * 4 + x) * 2 + lax.div(z, 4)) * 2 + core)

def aligned(index, multiple):
    return pl.multiple_of(index, multiple)

def comm_kernel(
    limit,
    act_a_hbm, dy_a_hbm, act_e_hbm, dy_e_hbm, w_a_hbm, m_a_hbm, v_a_hbm, w_e_hbm, m_e_hbm, v_e_hbm,
    g_hbm, f_hbm, full,
    act_a, dy_a, act_e, dy_e, w_a, m_a, v_a, w_e, m_e, v_e, g_out, f_out,
    lhs_a, lhs_e,
    cs, cr, own, s1, r1, own2, s2, r2,
    s3_a, s3_e, z3_a, z3_e, r3_a, r3_e,
    n_s, n_r,
    ws_a, ws_e, gr_a, gr_e, g3_a, g3_e, gt,
    send_sem, recv_sem, local_sem,
):
    z_lo = lax.axis_index("expert")
    dp = lax.axis_index("dp")
    core = lax.rem(dp, 2)
    z_hi = lax.rem(lax.div(dp, 2), 2)
    x = lax.rem(lax.div(dp, 4), 4)
    y = lax.div(dp, 16)
    z = z_hi * 4 + z_lo
    other = 1 - core
    peer = device_at(z, y, x, other)

    def zc_mate(dz, dc):
        oz = lax.rem(z + dz, 8)
        oc = core if dc == 0 else other
        return oz, oc

    def plane_mate(dy, dx):
        return device_at(z, lax.rem(y + dy, 4), lax.rem(x + dx, 4), core)

    def axis_mate(axis, d):
        return plane_mate(d, 0) if axis == 0 else plane_mate(0, d)

    place = (y, x)

    kept = []
    waited = []

    def keep(src, dst):
        copy = pltpu.make_async_copy(src, dst, local_sem.at[len(kept)])
        copy.start()
        kept.append(copy)
        return copy

    def need(copies):
        for copy in copies:
            copy.wait()
            waited.append(copy)

    sent = []
    arrived = []

    def send(src, dst, where):
        i = len(sent)
        copy = pltpu.make_async_remote_copy(
            src_ref=src, dst_ref=dst, send_sem=send_sem.at[i], recv_sem=recv_sem.at[i],
            device_id=where, device_id_type=MESH,
        )
        copy.start()
        sent.append(copy)
        return copy

    def arrive(copies):
        for copy in copies:
            copy.wait_recv()
            arrived.append(copy)

    def finish_all():
        arrive([copy for copy in sent if not any(copy is done for done in arrived)])
        for copy in kept[len(waited):]:
            copy.wait()
        for copy in sent:
            copy.wait_send()

    need_act = (keep(act_a_hbm, act_a), keep(act_e_hbm.at[0], act_e))
    need_dy = []
    for half in (other, core):
        for part in range(2):
            cols = pl.ds(aligned(half * HALF + part * PART, PART), PART)
            need_dy.append((
                keep(dy_a_hbm.at[:, cols], dy_a.at[:, cols]),
                keep(dy_e_hbm.at[0, :, cols], dy_e.at[:, cols]),
            ))
    need_state = [
        keep(src, dst)
        for src, dst in (
            (w_a_hbm, w_a), (m_a_hbm, m_a), (v_a_hbm, v_a), (w_e_hbm, w_e), (m_e_hbm, m_e), (v_e_hbm, v_e)
        )
    ]

    barrier = pltpu.get_barrier_semaphore()
    greeted = 0
    for dz in range(8):
        for dc in range(2):
            if dz or dc:
                oz, oc = zc_mate(dz, dc)
                pl.semaphore_signal(barrier, inc=1, device_id=device_at(oz, y, x, oc), device_id_type=MESH)
                greeted += 1
    for dy in range(4):
        for dx in range(4):
            if dy or dx:
                pl.semaphore_signal(barrier, inc=1, device_id=plane_mate(dy, dx), device_id_type=MESH)
                greeted += 1

    need(need_act)
    r0 = lax.broadcasted_iota(jnp.int32, (256, 256), 0)
    r1_ = lax.broadcasted_iota(jnp.int32, (256, 256), 1)
    pick = jnp.where(r0 == grouped(r1_), 1.0, 0.0).astype(BF16)
    lhs_a[...] = lax.dot_general(
        pick, act_a[...], (((1,), (1,)), ((), ())), preferred_element_type=F32
    ).astype(BF16)
    e0 = lax.broadcasted_iota(jnp.int32, (128, 128), 0)
    e1 = lax.broadcasted_iota(jnp.int32, (128, 128), 1)
    same = jnp.where(e0 == e1, 1.0, 0.0).astype(BF16)
    lhs_e[...] = lax.dot_general(
        same, act_e[...], (((1,), (1,)), ((), ())), preferred_element_type=F32
    ).astype(BF16)

    def terms(col):
        ga = jnp.dot(lhs_a[...], dy_a[:, pl.ds(col, STEP)], preferred_element_type=F32)
        ge = jnp.dot(lhs_e[...], dy_e[:, pl.ds(col, STEP)], preferred_element_type=F32)
        return ga.reshape(4, 4, 2, 8, STEP), ge.reshape(4, 4, 8, STEP)

    copies_c = []
    for part in range(2):
        def other_terms(i, carry):
            at = pl.ds(aligned(i * STEP, STEP), STEP)
            ga, ge = terms(aligned(other * HALF + part * PART + i * STEP, STEP))
            cs[part, :, :, 0:2, :, at] = ga.astype(BF16)
            cs[part, :, :, 2, :, at] = ge.astype(BF16)
            return carry

        need(need_dy[part])
        lax.fori_loop(0, PART // STEP, other_terms, 0)
        if part == 0:
            pl.semaphore_wait(barrier, greeted)
        copies_c.append(send(cs.at[part], cr.at[part], peer))

    def block(ref, part, second, first):
        return ref.at[part, second, first] if part == 0 else ref.at[part, first, second]

    order = (2, 1, 3, 0)
    copies_1 = []
    for part in range(2):
        arrive([copies_c[part]])
        need(need_dy[2 + part])

        def own_terms(i, carry):
            at = pl.ds(aligned(i * STEP, STEP), STEP)
            ga, ge = terms(aligned(core * HALF + part * PART + i * STEP, STEP))
            ga = ga + cr[part, :, :, 0:2, :, at].astype(F32)
            own[part, :, :, 0:2, :, at] = ga
            s1[part, :, :, 0:2, :, at] = ga.astype(BF16)
            ge = ge + cr[part, :, :, 2, :, at].astype(F32)
            own[part, :, :, 2, :, at] = ge
            s1[part, :, :, 2, :, at] = ge.astype(BF16)
            return carry

        lax.fori_loop(0, PART // STEP, own_terms, 0)
        first = 1 - part
        batches = {}
        for d in order:
            at = lax.rem(place[part] + d, 4)
            batches[d] = [
                send(
                    block(s1, part, at, lax.rem(place[first] + e, 4)),
                    r1.at[part, e - 1, at],
                    axis_mate(first, e),
                )
                for e in (2, 1, 3)
            ]
        copies_1.append(batches)

    copies_2 = [[], []]
    for d in order:
        for part in range(2):
            first = 1 - part
            at = lax.rem(place[part] + d, 4)
            arrive(copies_1[part][d])
            total = block(own, part, at, place[first])[...]
            for e in range(3):
                total = total + r1[part, e, at].astype(F32)
            if d:
                s2[part, d - 1] = total.astype(BF16)
                copies_2[part].append(send(s2.at[part, d - 1], r2.at[part, d - 1], axis_mate(part, d)))
            else:
                own2[part] = total

    for part in range(2):
        arrive(copies_2[part])
        total = own2[part]
        for d in range(3):
            total = total + r2[part, d].astype(F32)
        total_a = total[0:2].reshape(16, PART)
        total_e = total[2]
        for t in range(PROWS):
            lanes = slice(t * LANES, (t + 1) * LANES)
            s3_a[pl.ds(part * PROWS + t, 16, stride=ROWS), :] = total_a[:, lanes]
            s3_e[pl.ds(part * PROWS + t, 8, stride=ROWS), :] = total_e[:, lanes]
    z3_a[...] = s3_a[...].astype(BF16).reshape(16, ROWS, LANES)
    z3_e[...] = s3_e[...].astype(BF16).reshape(4, 2 * ROWS, LANES)

    z_order = (4, 3, 5, 2, 6, 1, 7, 0)
    batch = []
    for dz in z_order:
        for dc in range(2):
            if dz or dc:
                oz, oc = zc_mate(dz, dc)
                q = lax.rem(oz, 4) * 4 + lax.div(oz, 4) * 2 + oc
                batch.append(send(z3_a.at[q], r3_a.at[dc, dz], device_at(oz, y, x, oc)))
                if dz in (0, 4):
                    q = lax.div(oz, 4) * 2 + oc
                    batch.append(send(z3_e.at[q], r3_e.at[dc, dz // 4], device_at(oz, y, x, oc)))
    arrive(batch)

    my_q = z_lo * 4 + z_hi * 2 + core
    my_e = z_hi * 2 + core
    near = s3_a[pl.ds(aligned(my_q * ROWS, 8), ROWS), :]
    far = r3_a[1, 0].astype(F32)
    for dz in range(1, 8):
        near = near + r3_a[0, dz].astype(F32)
        far = far + r3_a[1, dz].astype(F32)
    near_at = pl.ds(aligned(core * ROWS, 8), ROWS)
    far_at = pl.ds(aligned(other * ROWS, 8), ROWS)
    g_out[0, near_at, :] = near
    g_out[0, far_at, :] = far
    near_e = s3_e[pl.ds(aligned(my_e * 2 * ROWS, 8), 2 * ROWS), :] + r3_e[0, 1].astype(F32)
    far_e = r3_e[1, 0].astype(F32) + r3_e[1, 1].astype(F32)
    for j in range(2):
        g_out[1 + j, near_at, :] = near_e[j * ROWS : (j + 1) * ROWS]
        g_out[1 + j, far_at, :] = far_e[j * ROWS : (j + 1) * ROWS]

    square = jnp.zeros((8, LANES), F32)
    for piece in (near, far, near_e, far_e):
        for i in range(piece.shape[0] // 8):
            part_of = piece[i * 8 : (i + 1) * 8]
            square = square + part_of * part_of
    n_s[0] = square
    batch = []
    for dz in z_order:
        for dc in range(2):
            if dz or dc:
                oz, oc = zc_mate(dz, dc)
                batch.append(send(n_s.at[0], n_r.at[0, dz * 2 + dc], device_at(oz, y, x, oc)))
    arrive(batch)
    for i in range(1, 16):
        square = square + n_r[0, i]
    n_s[1] = square
    batch = []
    for dy in order:
        for dx in order:
            if dy or dx:
                batch.append(send(n_s.at[1], n_r.at[1, dy * 4 + dx], plane_mate(dy, dx)))
    arrive(batch)
    for i in range(1, 16):
        square = square + n_r[1, i]
    norm = jnp.sqrt(jnp.sum(square, keepdims=True))
    factor = jnp.minimum(1.0, limit / (norm + 1e-06))
    f_out[...] = jnp.broadcast_to(factor, (8, LANES))

    need(need_state)
    keep(g_out, g_hbm)
    keep(f_out, f_hbm)
    weight_a = adamw(g_out[0], w_a[...], m_a[...], v_a[...], factor)[0].astype(BF16)
    for h in range(2):
        ws_a[h] = weight_a[h * ROWS : (h + 1) * ROWS]
    for j in range(2):
        rows = pl.ds(j, 2 * ROWS, stride=2)
        weight_e = adamw(g_out[1 + j], w_e[rows, :], m_e[rows, :], v_e[rows, :], factor)[0].astype(BF16)
        for h in range(2):
            ws_e[h, pl.ds(j * ROWS, ROWS), :] = weight_e[h * ROWS : (h + 1) * ROWS]

    batch = []
    for dz in z_order:
        for dc in range(2):
            if dz or dc:
                oz, oc = zc_mate(dz, dc)
                batch.append(send(ws_a.at[oc], gr_a.at[my_q], device_at(oz, y, x, oc)))
                if dz in (0, 4):
                    batch.append(send(ws_e.at[oc], gr_e.at[my_e], device_at(oz, y, x, oc)))
    gr_a[my_q] = ws_a[core]
    gr_e[my_e] = ws_e[core]
    arrive(batch)
    g3_a[...] = gr_a[...].astype(F32).reshape(16 * ROWS, LANES)
    g3_e[...] = gr_e[...].astype(F32).reshape(8 * ROWS, LANES)
    for part in range(2):
        for t in range(PROWS):
            lanes = pl.ds(t * LANES, LANES)
            tile_a = g3_a[pl.ds(part * PROWS + t, 16, stride=ROWS), :].astype(BF16)
            gt[part, y, x, 0:2, :, lanes] = tile_a.reshape(2, 8, LANES)
            gt[part, y, x, 2, :, lanes] = g3_e[pl.ds(part * PROWS + t, 8, stride=ROWS), :].astype(BF16)

    def spread(part, at):
        here = block(gt, part, at, place[1 - part])
        return {e: send(here, here, axis_mate(1 - part, e)) for e in (2, 1, 3)}

    def deliver(part, at, first_at):
        src = block(gt, part, at, first_at)
        dst = block(full.at[core], part, at, first_at)
        send(src, dst, peer)
        keep(src, dst)

    copies_2 = [{}, {}]
    for part in range(2):
        here = gt.at[part, y, x]
        copies_2[part] = {d: send(here, here, axis_mate(part, d)) for d in (2, 1, 3)}
    copies_1 = [{0: spread(part, place[part])} for part in range(2)]
    for part in range(2):
        deliver(part, place[part], place[1 - part])
    for d in (1, 3, 2):
        for part in range(2):
            at = lax.rem(place[part] + 4 - d, 4)
            arrive([copies_2[part][d]])
            copies_1[part][d] = spread(part, at)
            deliver(part, at, place[1 - part])
    for d in (0, 1, 3, 2):
        for part in range(2):
            at = lax.rem(place[part] + 4 - d, 4)
            for e in (1, 3, 2):
                arrive([copies_1[part][d][e]])
                deliver(part, at, lax.rem(place[1 - part] + 4 - e, 4))
    finish_all()

def finish_kernel(
    full, g, f, w_a, m_a, v_a, w_e, m_e, v_e,
    wa_o, ma_o, va_o, we_o, me_o, ve_o, attn_o, exp_o, pick,
):
    @pl.when(pl.program_id(0) == 0)
    def _():
        r0 = lax.broadcasted_iota(jnp.int32, (256, 256), 0)
        r1 = lax.broadcasted_iota(jnp.int32, (256, 256), 1)
        pick[...] = jnp.where(grouped(r0) == r1, 1.0, 0.0).astype(BF16)
        factor = f[0:1, 0:1]
        new = adamw(g[0], w_a[...], m_a[...], v_a[...], factor)
        for ref, value in zip((wa_o, ma_o, va_o), new):
            ref[...] = value
        for j in range(2):
            rows = pl.ds(j, 2 * ROWS, stride=2)
            new = adamw(g[1 + j], w_e[rows, :], m_e[rows, :], v_e[rows, :], factor)
            for ref, value in zip((we_o, me_o, ve_o), new):
                ref[rows, :] = value

    gathered = full[0, :, 0:2].reshape(256, WIDE)
    attn_o[...] = jnp.dot(pick[...], gathered, preferred_element_type=F32).astype(BF16)
    exp_o[0] = full[0, :, 2].reshape(128, WIDE)

def comm_part(act_attn, dy_attn, act_exp, dy_exp, w_attn, m_attn, v_attn, w_exp, m_exp, v_exp):
    width = w_attn.shape[1]
    total_params = width * (act_attn.shape[1] + lax.axis_size("expert") * act_exp.shape[2])
    limit = 0.5 * math.sqrt(total_params)
    attn_state = [v.reshape(2 * ROWS, LANES) for v in (w_attn, m_attn, v_attn)]
    exp_state = [
        v.reshape(2, 2 * ROWS, LANES).transpose(1, 0, 2).reshape(4 * ROWS, LANES)
        for v in (w_exp, m_exp, v_exp)
    ]
    hbm = pl.BlockSpec(memory_space=pltpu.HBM)
    n_send = 170

    def blocks(dtype, *lead):
        return pltpu.VMEM(lead + (3, 8, PART), dtype)

    outs = pl.pallas_call(
        lambda *refs: comm_kernel(limit, *refs),
        out_shape=(
            jax.ShapeDtypeStruct((3, 2 * ROWS, LANES), F32),
            jax.ShapeDtypeStruct((8, LANES), F32),
            jax.ShapeDtypeStruct((2, 2, 4, 4, 3, 8, PART), BF16),
        ),
        in_specs=[hbm] * 10,
        out_specs=(hbm,) * 3,
        scratch_shapes=[
            pltpu.VMEM((256, 256), BF16),
            pltpu.VMEM((256, 4 * PART), BF16),
            pltpu.VMEM((128, 128), BF16),
            pltpu.VMEM((128, 4 * PART), BF16),
            *[pltpu.VMEM((2 * ROWS, LANES), F32)] * 3,
            *[pltpu.VMEM((4 * ROWS, LANES), F32)] * 3,
            pltpu.VMEM((3, 2 * ROWS, LANES), F32),
            pltpu.VMEM((8, LANES), F32),
            pltpu.VMEM((256, 256), BF16),
            pltpu.VMEM((128, 128), BF16),
            blocks(BF16, 2, 4, 4),
            blocks(BF16, 2, 4, 4),
            blocks(F32, 2, 4, 4),
            blocks(BF16, 2, 4, 4),
            blocks(BF16, 2, 3, 4),
            blocks(F32, 2),
            blocks(BF16, 2, 3),
            blocks(BF16, 2, 3),
            pltpu.VMEM((16 * ROWS, LANES), F32),
            pltpu.VMEM((8 * ROWS, LANES), F32),
            pltpu.VMEM((16, ROWS, LANES), BF16),
            pltpu.VMEM((4, 2 * ROWS, LANES), BF16),
            pltpu.VMEM((2, 8, ROWS, LANES), BF16),
            pltpu.VMEM((2, 2, 2 * ROWS, LANES), BF16),
            pltpu.VMEM((2, 8, LANES), F32),
            pltpu.VMEM((2, 16, 8, LANES), F32),
            pltpu.VMEM((2, ROWS, LANES), BF16),
            pltpu.VMEM((2, 2 * ROWS, LANES), BF16),
            pltpu.VMEM((16, ROWS, LANES), BF16),
            pltpu.VMEM((4, 2 * ROWS, LANES), BF16),
            pltpu.VMEM((16 * ROWS, LANES), F32),
            pltpu.VMEM((8 * ROWS, LANES), F32),
            blocks(BF16, 2, 4, 4),
            pltpu.SemaphoreType.DMA((n_send,)),
            pltpu.SemaphoreType.DMA((n_send,)),
            pltpu.SemaphoreType.DMA((60,)),
        ],
        compiler_params=pltpu.CompilerParams(
            collective_id=0, has_side_effects=True, vmem_limit_bytes=63 * 1024 * 1024
        ),
    )(act_attn, dy_attn, act_exp, dy_exp, *attn_state, *exp_state)
    return outs, attn_state, exp_state

def body(act_attn, dy_attn, act_exp, dy_exp, *state):
    width = dy_attn.shape[1]
    (g, f, full), attn_state, exp_state = comm_part(act_attn, dy_attn, act_exp, dy_exp, *state)
    steps = width // WIDE
    per_part = PART // WIDE
    whole = lambda shape: pl.BlockSpec(shape, lambda i: (0,) * len(shape))
    a_shape, e_shape = (2 * ROWS, LANES), (4 * ROWS, LANES)
    outs = pl.pallas_call(
        finish_kernel,
        grid=(steps,),
        out_shape=(
            *[jax.ShapeDtypeStruct(a_shape, F32)] * 3,
            *[jax.ShapeDtypeStruct(e_shape, F32)] * 3,
            jax.ShapeDtypeStruct((256, width), BF16),
            jax.ShapeDtypeStruct((1, 128, width), BF16),
        ),
        in_specs=[
            pl.BlockSpec((1, 16, 3, 8, WIDE), lambda i: (i // per_part, 0, 0, 0, i % per_part)),
            whole((3, 2 * ROWS, LANES)),
            whole((8, LANES)),
            *[whole(a_shape)] * 3,
            *[whole(e_shape)] * 3,
        ],
        out_specs=(
            *[whole(a_shape)] * 3,
            *[whole(e_shape)] * 3,
            pl.BlockSpec((256, WIDE), lambda i: (0, i)),
            pl.BlockSpec((1, 128, WIDE), lambda i: (0, 0, i)),
        ),
        scratch_shapes=[pltpu.VMEM((256, 256), BF16)],
        compiler_params=pltpu.CompilerParams(vmem_limit_bytes=63 * 1024 * 1024),
    )(full.reshape(4, 16, 3, 8, PART), g, f, *attn_state, *exp_state)
    attn_new = [v.reshape(1, width) for v in outs[:3]]
    exp_new = [
        v.reshape(2 * ROWS, 2, LANES).transpose(1, 0, 2).reshape(1, 2, width) for v in outs[3:6]
    ]
    return (*attn_new, *exp_new, outs[6], outs[7])

def solution(mesh):
    rows = P(("expert", "dp"), None)
    owned = P("expert", "dp", None)
    return jax.shard_map(
        body,
        mesh=mesh,
        in_specs=(rows, rows, owned, owned, rows, rows, rows, owned, owned, owned),
        out_specs=(rows, rows, rows, owned, owned, owned, P(), P("expert", None, None)),
        check_vma=False,
    )
```

```python
import math

import jax
import jax.numpy as jnp
from jax import lax
from jax.experimental import pallas as pl
from jax.experimental.pallas import tpu as pltpu
from jax.sharding import PartitionSpec as P

beta_first = 0.9
beta_second = 0.95
bias_first = 1.0 - 0.9**10
bias_second = 1.0 - 0.95**10
learn_rate = 0.01
decay_rate = 0.1
adam_eps = 1e-08

MESH = pl.DeviceIdType.MESH
F32 = jnp.float32
BF16 = jnp.bfloat16
HALF = 3072
PART = 1536
LANES = 128
ROWS = HALF // LANES
PROWS = PART // LANES
SUB = 768
SROWS = SUB // LANES
WIDE = 768


def adamw(grad, weight, moment, second, factor):
    scaled = factor * grad
    moment_new = beta_first * moment + (1.0 - beta_first) * scaled
    second_new = beta_second * second + (1.0 - beta_second) * scaled * scaled
    update = moment_new / bias_first / (jnp.sqrt(second_new / bias_second) + adam_eps)
    weight_new = weight - learn_rate * (update + decay_rate * weight)
    return (weight_new, moment_new, second_new)


def grouped(row):
    low = row & 3
    x = (row >> 2) & 3
    y = (row >> 4) & 3
    z_lo = row >> 6
    return ((y * 4 + x) * 4 + z_lo) * 4 + low


def device_at(z, y, x, core):
    return (lax.rem(z, 4), ((y * 4 + x) * 2 + lax.div(z, 4)) * 2 + core)


def aligned(index, multiple):
    return pl.multiple_of(index, multiple)


def comm_kernel(
    limit,
    act_a_hbm, dy_a_hbm, act_e_hbm, dy_e_hbm, w_a_hbm, m_a_hbm, v_a_hbm, w_e_hbm, m_e_hbm, v_e_hbm,
    g_hbm, f_hbm, full,
    act_a, dy_a, act_e, dy_e, w_e, m_e, v_e, g_out, f_out,
    lhs_a, lhs_e, st_a, st_e, pf_a, pf_e,
    cs, cr, own, s1, r1, own2, s2, r2,
    s3_a, s3_e, z3_a, z3_e, r3_a, r3_e,
    n_s, n_r,
    ws_a, ws_e, gr_a, gr_e, g3_a, g3_e, gt,
    send_sem, recv_sem, local_sem,
):
    z_lo = lax.axis_index("expert")
    dp = lax.axis_index("dp")
    core = lax.rem(dp, 2)
    z_hi = lax.rem(lax.div(dp, 2), 2)
    x = lax.rem(lax.div(dp, 4), 4)
    y = lax.div(dp, 16)
    z = z_hi * 4 + z_lo
    other = 1 - core
    peer = device_at(z, y, x, other)

    def zc_mate(dz, dc):
        oz = lax.rem(z + dz, 8)
        oc = core if dc == 0 else other
        return oz, oc

    def plane_mate(dy, dx):
        return device_at(z, lax.rem(y + dy, 4), lax.rem(x + dx, 4), core)

    def axis_mate(axis, d):
        return plane_mate(d, 0) if axis == 0 else plane_mate(0, d)

    place = (y, x)

    kept = []
    waited = []

    def keep(src, dst):
        copy = pltpu.make_async_copy(src, dst, local_sem.at[len(kept)])
        copy.start()
        kept.append(copy)
        return copy

    def need(copies):
        for copy in copies:
            copy.wait()
            waited.append(copy)

    sent = []
    arrived = []

    def send(src, dst, where):
        i = len(sent)
        copy = pltpu.make_async_remote_copy(
            src_ref=src, dst_ref=dst, send_sem=send_sem.at[i], recv_sem=recv_sem.at[i],
            device_id=where, device_id_type=MESH,
        )
        copy.start()
        sent.append(copy)
        return copy

    def arrive(copies):
        for copy in copies:
            copy.wait_recv()
            arrived.append(copy)

    def finish_all():
        arrive([copy for copy in sent if not any(copy is done for done in arrived)])
        for copy in [copy for copy in kept if not any(copy is done for done in waited)]:
            copy.wait()
        for copy in sent:
            copy.wait_send()

    need_act = (keep(act_a_hbm, act_a), keep(act_e_hbm.at[0], act_e))
    need_dy = {}
    for half in range(2):
        for s in range(4):
            cols = pl.ds(aligned((other if half == 0 else core) * HALF + s * SUB, SUB), SUB)
            need_dy[half, s] = (
                keep(dy_a_hbm.at[:, cols], dy_a.at[:, cols]),
                keep(dy_e_hbm.at[0, :, cols], dy_e.at[:, cols]),
            )
    need_state = [
        keep(src, st_a.at[:, pl.ds(k * ROWS, ROWS)]) for k, src in enumerate((w_a_hbm, m_a_hbm, v_a_hbm))
    ] + [keep(src, dst) for src, dst in ((w_e_hbm, w_e), (m_e_hbm, m_e), (v_e_hbm, v_e))]

    barrier = pltpu.get_barrier_semaphore()
    greeted = 0
    for dz in range(8):
        for dc in range(2):
            if dz or dc:
                oz, oc = zc_mate(dz, dc)
                pl.semaphore_signal(barrier, inc=1, device_id=device_at(oz, y, x, oc), device_id_type=MESH)
                greeted += 1
    for dy in range(4):
        for dx in range(4):
            if dy or dx:
                pl.semaphore_signal(barrier, inc=1, device_id=plane_mate(dy, dx), device_id_type=MESH)
                greeted += 1

    r0 = lax.broadcasted_iota(jnp.int32, (256, 256), 0)
    r1_ = lax.broadcasted_iota(jnp.int32, (256, 256), 1)
    pick = jnp.where(r0 == grouped(r1_), 1.0, 0.0).astype(BF16)
    need(need_act)
    lhs_a[...] = lax.dot_general(
        pick, act_a[...], (((1,), (1,)), ((), ())), preferred_element_type=F32
    ).astype(BF16)
    e0 = lax.broadcasted_iota(jnp.int32, (128, 128), 0)
    e1 = lax.broadcasted_iota(jnp.int32, (128, 128), 1)
    same = jnp.where(e0 == e1, 1.0, 0.0).astype(BF16)
    lhs_e[...] = lax.dot_general(
        same, act_e[...], (((1,), (1,)), ((), ())), preferred_element_type=F32
    ).astype(BF16)

    def terms(half, s):
        need(need_dy[half, s])
        cols = pl.ds(aligned((other if half == 0 else core) * HALF + s * SUB, SUB), SUB)
        ga = jnp.dot(lhs_a[...], dy_a[:, cols], preferred_element_type=F32)
        ge = jnp.dot(lhs_e[...], dy_e[:, cols], preferred_element_type=F32)
        return ga.reshape(4, 4, 2, 8, SUB), ge.reshape(4, 4, 8, SUB)

    def block(ref, part, second, first):
        return ref.at[part, second, first] if part % 2 == 0 else ref.at[part, first, second]

    order = (2, 1, 3, 0)
    copies_c, copies_1 = {}, {}

    def give(s):
        ga, ge = terms(0, s)
        cs[s, :, :, 0:2] = ga.astype(BF16)
        cs[s, :, :, 2] = ge.astype(BF16)
        if s == 0:
            pl.semaphore_wait(barrier, greeted)
        copies_c[s] = send(cs.at[s], cr.at[s], peer)

    def take(s):
        ga, ge = terms(1, s)
        own[s, :, :, 0:2] = ga
        own[s, :, :, 2] = ge
        arrive([copies_c[s]])
        for b in range(4):
            both = own[s, b] + cr[s, b].astype(F32)
            own[s, b] = both
            s1[s, b] = both.astype(BF16)
        first = 1 - s % 2
        if s < 2:
            copies_1[s] = []
            for e in (2, 1, 3):
                to = lax.rem(place[first] + e, 4)
                src = s1.at[s, :, to] if s % 2 == 0 else s1.at[s, to]
                copies_1[s].append(send(src, r1.at[s, e - 1], axis_mate(first, e)))
        else:
            for d in order:
                at = lax.rem(place[s % 2] + d, 4)
                copies_1[s, d] = [
                    send(
                        block(s1, s, at, lax.rem(place[first] + e, 4)),
                        r1.at[s, e - 1, at],
                        axis_mate(first, e),
                    )
                    for e in (2, 1, 3)
                ]

    give(0)
    z_order = (4, 3, 5, 2, 6, 1, 7, 0)
    my_q = z_lo * 4 + z_hi * 2 + core
    my_e = z_hi * 2 + core
    need(need_state)
    for h in range(2):
        for j in range(2):
            for k, state in enumerate((w_e, m_e, v_e)):
                st_e[h, pl.ds((j * 3 + k) * ROWS, ROWS), :] = state[pl.ds(h * 2 * ROWS + j, ROWS, stride=2), :]
    pf_at_a = pl.ds(aligned(my_q * 3 * ROWS, 8), 3 * ROWS)
    pf_at_e = pl.ds(aligned(my_e * 6 * ROWS, 8), 6 * ROWS)
    copies_pf = []
    for dz in z_order:
        for dc in range(2):
            if dz or dc:
                oz, oc = zc_mate(dz, dc)
                copies_pf.append(send(st_a.at[oc], pf_a.at[pf_at_a], device_at(oz, y, x, oc)))
                if dz in (0, 4):
                    copies_pf.append(send(st_e.at[oc], pf_e.at[pf_at_e], device_at(oz, y, x, oc)))
    pf_a[pf_at_a, :] = st_a[core]
    pf_e[pf_at_e, :] = st_e[core]

    give(1)
    take(0)
    take(1)
    give(2)
    give(3)
    take(2)
    take(3)

    copies_2 = {s: [] for s in range(4)}

    def pass_on(s, d):
        at = lax.rem(place[s % 2] + d, 4)
        total = block(own, s, at, place[1 - s % 2])[...]
        for e in range(3):
            total = total + r1[s, e, at].astype(F32)
        if d:
            s2[s, d - 1] = total.astype(BF16)
            copies_2[s].append(send(s2.at[s, d - 1], r2.at[s, d - 1], axis_mate(s % 2, d)))
        else:
            own2[s] = total

    for s in (0, 1):
        arrive(copies_1[s])
        for d in order:
            pass_on(s, d)
    for d in order:
        for s in (2, 3):
            arrive(copies_1[s, d])
            pass_on(s, d)

    for s in range(4):
        arrive(copies_2[s])
        total = own2[s]
        for d in range(3):
            total = total + r2[s, d].astype(F32)
        total_a = total[0:2].reshape(16, SUB)
        total_e = total[2]
        for t in range(SROWS):
            lanes = slice(t * LANES, (t + 1) * LANES)
            s3_a[pl.ds(s * SROWS + t, 16, stride=ROWS), :] = total_a[:, lanes]
            s3_e[pl.ds(s * SROWS + t, 8, stride=ROWS), :] = total_e[:, lanes]
    z3_a[...] = s3_a[...].astype(BF16).reshape(16, ROWS, LANES)
    z3_e[...] = s3_e[...].astype(BF16).reshape(4, 2 * ROWS, LANES)

    batch = []
    for dz in z_order:
        for dc in range(2):
            if dz or dc:
                oz, oc = zc_mate(dz, dc)
                q = lax.rem(oz, 4) * 4 + lax.div(oz, 4) * 2 + oc
                batch.append(send(z3_a.at[q], r3_a.at[dc, dz], device_at(oz, y, x, oc)))
                if dz in (0, 4):
                    q = lax.div(oz, 4) * 2 + oc
                    batch.append(send(z3_e.at[q], r3_e.at[dc, dz // 4], device_at(oz, y, x, oc)))
    arrive(batch)

    near = s3_a[pl.ds(aligned(my_q * ROWS, 8), ROWS), :]
    far = r3_a[1, 0].astype(F32)
    for dz in range(1, 8):
        near = near + r3_a[0, dz].astype(F32)
        far = far + r3_a[1, dz].astype(F32)
    near_at = pl.ds(aligned(core * ROWS, 8), ROWS)
    far_at = pl.ds(aligned(other * ROWS, 8), ROWS)
    g_out[0, near_at, :] = near
    g_out[0, far_at, :] = far
    near_e = s3_e[pl.ds(aligned(my_e * 2 * ROWS, 8), 2 * ROWS), :] + r3_e[0, 1].astype(F32)
    far_e = r3_e[1, 0].astype(F32) + r3_e[1, 1].astype(F32)
    for j in range(2):
        g_out[1 + j, near_at, :] = near_e[j * ROWS : (j + 1) * ROWS]
        g_out[1 + j, far_at, :] = far_e[j * ROWS : (j + 1) * ROWS]

    square = jnp.zeros((8, LANES), F32)
    for piece in (near, far, near_e, far_e):
        for i in range(piece.shape[0] // 8):
            part_of = piece[i * 8 : (i + 1) * 8]
            square = square + part_of * part_of
    n_s[0] = square
    batch = []
    for dz in z_order:
        for dc in range(2):
            if dz or dc:
                oz, oc = zc_mate(dz, dc)
                batch.append(send(n_s.at[0], n_r.at[0, dz * 2 + dc], device_at(oz, y, x, oc)))
    ws_a[core] = near.astype(BF16)
    ws_a[other] = far.astype(BF16)
    ws_e[core] = near_e.astype(BF16)
    ws_e[other] = far_e.astype(BF16)
    copies_g = []
    for dz in z_order:
        for dc in range(2):
            if dz or dc:
                oz, oc = zc_mate(dz, dc)
                copies_g.append(send(ws_a.at[oc], gr_a.at[my_q], device_at(oz, y, x, oc)))
                if dz in (0, 4):
                    copies_g.append(send(ws_e.at[oc], gr_e.at[my_e], device_at(oz, y, x, oc)))
    gr_a[my_q] = ws_a[core]
    gr_e[my_e] = ws_e[core]
    keep(g_out, g_hbm)
    arrive(batch)
    for i in range(1, 16):
        square = square + n_r[0, i]
    n_s[1] = square
    batch = []
    for dy in order:
        for dx in order:
            if dy or dx:
                batch.append(send(n_s.at[1], n_r.at[1, dy * 4 + dx], plane_mate(dy, dx)))
    arrive(copies_g)
    g3_a[...] = gr_a[...].astype(F32).reshape(16 * ROWS, LANES)
    g3_e[...] = gr_e[...].astype(F32).reshape(8 * ROWS, LANES)
    arrive(copies_pf)
    arrive(batch)
    for i in range(1, 16):
        square = square + n_r[1, i]
    norm = jnp.sqrt(jnp.sum(square, keepdims=True))
    factor = jnp.minimum(1.0, limit / (norm + 1e-06))
    f_out[...] = jnp.broadcast_to(factor, (8, LANES))
    keep(f_out, f_hbm)

    def new_tile(rows, grad, state, t):
        values = [state[pl.ds(k * ROWS + t, rows, stride=3 * ROWS), :] for k in range(3)]
        return adamw(grad[pl.ds(t, rows, stride=ROWS), :], *values, factor)[0].astype(BF16)

    for part in range(2):
        for t in range(PROWS):
            lanes = pl.ds(t * LANES, LANES)
            gt[part, y, x, 0:2, :, lanes] = new_tile(16, g3_a, pf_a, part * PROWS + t).reshape(2, 8, LANES)
            gt[part, y, x, 2, :, lanes] = new_tile(8, g3_e, pf_e, part * PROWS + t)

    def spread(part, at):
        here = block(gt, part, at, place[1 - part])
        return {e: send(here, here, axis_mate(1 - part, e)) for e in (2, 1, 3)}

    def deliver(part, at, first_at):
        src = block(gt, part, at, first_at)
        dst = block(full.at[core], part, at, first_at)
        send(src, dst, peer)
        keep(src, dst)

    copies_2 = [{}, {}]
    for part in range(2):
        here = gt.at[part, y, x]
        copies_2[part] = {d: send(here, here, axis_mate(part, d)) for d in (2, 1, 3)}
    copies_1 = [{0: spread(part, place[part])} for part in range(2)]
    for part in range(2):
        deliver(part, place[part], place[1 - part])
    for d in (1, 3, 2):
        for part in range(2):
            at = lax.rem(place[part] + 4 - d, 4)
            arrive([copies_2[part][d]])
            copies_1[part][d] = spread(part, at)
            deliver(part, at, place[1 - part])
    for d in (0, 1, 3, 2):
        for part in range(2):
            at = lax.rem(place[part] + 4 - d, 4)
            for e in (1, 3, 2):
                arrive([copies_1[part][d][e]])
                deliver(part, at, lax.rem(place[1 - part] + 4 - e, 4))
    finish_all()


def finish_kernel(
    full, g_hbm, f_hbm, w_a_hbm, m_a_hbm, v_a_hbm, w_e_hbm, m_e_hbm, v_e_hbm,
    wa_o, ma_o, va_o, we_o, me_o, ve_o, attn_o, exp_o,
    got, attn, g, f, st_a, st_e, new_a, new_e, pick, in_sem, out_sem, small_sem,
):
    reads = []
    for i in range(2 * HALF // WIDE):
        half, at = divmod(i * WIDE, PART)
        reads.append(pltpu.make_async_copy(full.at[half, :, :, :, pl.ds(at, WIDE)], got.at[i], in_sem.at[i]))
    pairs = [(g_hbm, g), (f_hbm, f)]
    pairs += [(ref, st_a.at[k]) for k, ref in enumerate((w_a_hbm, m_a_hbm, v_a_hbm))]
    pairs += [(ref, st_e.at[k]) for k, ref in enumerate((w_e_hbm, m_e_hbm, v_e_hbm))]
    small = [pltpu.make_async_copy(src, dst, small_sem.at[k]) for k, (src, dst) in enumerate(pairs)]
    for copy in reads[:2] + small + reads[2:]:
        copy.start()
    r0 = lax.broadcasted_iota(jnp.int32, (256, 256), 0)
    r1 = lax.broadcasted_iota(jnp.int32, (256, 256), 1)
    pick[...] = jnp.where(grouped(r0) == r1, 1.0, 0.0).astype(BF16)

    writes = []

    def write(src, dst):
        copy = pltpu.make_async_copy(src, dst, out_sem.at[len(writes)])
        copy.start()
        writes.append(copy)

    for i, copy in enumerate(reads):
        copy.wait()
        cols = pl.ds(i * WIDE, WIDE)
        write(got.at[i, :, 2], exp_o.at[:, :, cols])
        gathered = got[i, :, 0:2].reshape(256, WIDE)
        attn[i] = jnp.dot(pick[...], gathered, preferred_element_type=F32).astype(BF16)
        write(attn.at[i], attn_o.at[:, cols])
        if i == 1:
            for one in small:
                one.wait()
            factor = f[0:1, 0:1]
            new = adamw(g[0], st_a[0], st_a[1], st_a[2], factor)
            for k, ref in enumerate((wa_o, ma_o, va_o)):
                new_a[k] = new[k]
                write(new_a.at[k], ref)
            for j in range(2):
                rows = pl.ds(j, 2 * ROWS, stride=2)
                new = adamw(g[1 + j], *[st_e[k, rows, :] for k in range(3)], factor)
                for k in range(3):
                    new_e[k, rows, :] = new[k]
            for k, ref in enumerate((we_o, me_o, ve_o)):
                write(new_e.at[k], ref)
    for copy in writes:
        copy.wait()


def comm_part(act_attn, dy_attn, act_exp, dy_exp, w_attn, m_attn, v_attn, w_exp, m_exp, v_exp):
    width = w_attn.shape[1]
    total_params = width * (act_attn.shape[1] + lax.axis_size("expert") * act_exp.shape[2])
    limit = 0.5 * math.sqrt(total_params)
    attn_state = [v.reshape(2, ROWS, LANES) for v in (w_attn, m_attn, v_attn)]
    exp_state = [
        v.reshape(2, 2 * ROWS, LANES).transpose(1, 0, 2).reshape(4 * ROWS, LANES)
        for v in (w_exp, m_exp, v_exp)
    ]
    hbm = pl.BlockSpec(memory_space=pltpu.HBM)
    n_send = 200

    def blocks(dtype, *lead, width=SUB):
        return pltpu.VMEM(lead + (3, 8, width), dtype)

    outs = pl.pallas_call(
        lambda *refs: comm_kernel(limit, *refs),
        out_shape=(
            jax.ShapeDtypeStruct((3, 2 * ROWS, LANES), F32),
            jax.ShapeDtypeStruct((8, LANES), F32),
            jax.ShapeDtypeStruct((2, 2, 4, 4, 3, 8, PART), BF16),
        ),
        in_specs=[hbm] * 10,
        out_specs=(hbm,) * 3,
        scratch_shapes=[
            pltpu.VMEM((256, 256), BF16),
            pltpu.VMEM((256, 4 * PART), BF16),
            pltpu.VMEM((128, 128), BF16),
            pltpu.VMEM((128, 4 * PART), BF16),
            *[pltpu.VMEM((4 * ROWS, LANES), F32)] * 3,
            pltpu.VMEM((3, 2 * ROWS, LANES), F32),
            pltpu.VMEM((8, LANES), F32),
            pltpu.VMEM((256, 256), BF16),
            pltpu.VMEM((128, 128), BF16),
            pltpu.VMEM((2, 3 * ROWS, LANES), F32),
            pltpu.VMEM((2, 6 * ROWS, LANES), F32),
            pltpu.VMEM((16 * 3 * ROWS, LANES), F32),
            pltpu.VMEM((8 * 3 * ROWS, LANES), F32),
            blocks(BF16, 4, 4, 4),
            blocks(BF16, 4, 4, 4),
            blocks(F32, 4, 4, 4),
            blocks(BF16, 4, 4, 4),
            blocks(BF16, 4, 3, 4),
            blocks(F32, 4),
            blocks(BF16, 4, 3),
            blocks(BF16, 4, 3),
            pltpu.VMEM((16 * ROWS, LANES), F32),
            pltpu.VMEM((8 * ROWS, LANES), F32),
            pltpu.VMEM((16, ROWS, LANES), BF16),
            pltpu.VMEM((4, 2 * ROWS, LANES), BF16),
            pltpu.VMEM((2, 8, ROWS, LANES), BF16),
            pltpu.VMEM((2, 2, 2 * ROWS, LANES), BF16),
            pltpu.VMEM((2, 8, LANES), F32),
            pltpu.VMEM((2, 16, 8, LANES), F32),
            pltpu.VMEM((2, ROWS, LANES), BF16),
            pltpu.VMEM((2, 2 * ROWS, LANES), BF16),
            pltpu.VMEM((16, ROWS, LANES), BF16),
            pltpu.VMEM((4, 2 * ROWS, LANES), BF16),
            pltpu.VMEM((16 * ROWS, LANES), F32),
            pltpu.VMEM((8 * ROWS, LANES), F32),
            blocks(BF16, 2, 4, 4, width=PART),
            pltpu.SemaphoreType.DMA((n_send,)),
            pltpu.SemaphoreType.DMA((n_send,)),
            pltpu.SemaphoreType.DMA((80,)),
        ],
        compiler_params=pltpu.CompilerParams(
            collective_id=0, has_side_effects=True, vmem_limit_bytes=63 * 1024 * 1024
        ),
    )(act_attn, dy_attn, act_exp, dy_exp, *attn_state, *exp_state)
    return outs, attn_state, exp_state


def body(act_attn, dy_attn, act_exp, dy_exp, *state):
    width = dy_attn.shape[1]
    (g, f, full), attn_state, exp_state = comm_part(act_attn, dy_attn, act_exp, dy_exp, *state)
    a_shape, e_shape = (2 * ROWS, LANES), (4 * ROWS, LANES)
    steps = width // WIDE
    hbm = pl.BlockSpec(memory_space=pltpu.HBM)
    outs = pl.pallas_call(
        finish_kernel,
        out_shape=(
            *[jax.ShapeDtypeStruct(a_shape, F32)] * 3,
            *[jax.ShapeDtypeStruct(e_shape, F32)] * 3,
            jax.ShapeDtypeStruct((256, width), BF16),
            jax.ShapeDtypeStruct((16, 8, width), BF16),
        ),
        in_specs=[hbm] * 9,
        out_specs=(hbm,) * 8,
        scratch_shapes=[
            pltpu.VMEM((steps, 16, 3, 8, WIDE), BF16),
            pltpu.VMEM((steps, 256, WIDE), BF16),
            pltpu.VMEM((3, 2 * ROWS, LANES), F32),
            pltpu.VMEM((8, LANES), F32),
            pltpu.VMEM((3,) + a_shape, F32),
            pltpu.VMEM((3,) + e_shape, F32),
            pltpu.VMEM((3,) + a_shape, F32),
            pltpu.VMEM((3,) + e_shape, F32),
            pltpu.VMEM((256, 256), BF16),
            pltpu.SemaphoreType.DMA((steps,)),
            pltpu.SemaphoreType.DMA((2 * steps + 6,)),
            pltpu.SemaphoreType.DMA((8,)),
        ],
        compiler_params=pltpu.CompilerParams(vmem_limit_bytes=63 * 1024 * 1024),
    )(full.reshape(4, 16, 3, 8, PART), g, f, *[v.reshape(a_shape) for v in attn_state], *exp_state)
    attn_new = [v.reshape(1, width) for v in outs[:3]]
    exp_new = [
        v.reshape(2 * ROWS, 2, LANES).transpose(1, 0, 2).reshape(1, 2, width) for v in outs[3:6]
    ]
    return (*attn_new, *exp_new, outs[6], outs[7].reshape(1, 128, width))


def solution(mesh):
    rows = P(("expert", "dp"), None)
    owned = P("expert", "dp", None)
    return jax.shard_map(
        body,
        mesh=mesh,
        in_specs=(rows, rows, owned, owned, rows, rows, rows, owned, owned, owned),
        out_specs=(rows, rows, rows, owned, owned, owned, P(), P("expert", None, None)),
        check_vma=False,
    )
```

```python
import math

import jax
import jax.numpy as jnp
from jax import lax
from jax.experimental import pallas as pl
from jax.experimental.pallas import tpu as pltpu
from jax.sharding import PartitionSpec as P

beta_first = 0.9
beta_second = 0.95
bias_first = 1.0 - 0.9**10
bias_second = 1.0 - 0.95**10
learn_rate = 0.01
decay_rate = 0.1
adam_eps = 1e-08

MESH = pl.DeviceIdType.MESH
F32 = jnp.float32
BF16 = jnp.bfloat16
HALF = 3072
PART = 1536
LANES = 128
ROWS = HALF // LANES
PROWS = PART // LANES
SUB = 768
SROWS = SUB // LANES


def adamw(grad, weight, moment, second, factor):
    scaled = factor * grad
    moment_new = beta_first * moment + (1.0 - beta_first) * scaled
    second_new = beta_second * second + (1.0 - beta_second) * scaled * scaled
    update = moment_new / bias_first / (jnp.sqrt(second_new / bias_second) + adam_eps)
    weight_new = weight - learn_rate * (update + decay_rate * weight)
    return (weight_new, moment_new, second_new)


def grouped(row):
    low = row & 3
    x = (row >> 2) & 3
    y = (row >> 4) & 3
    z_lo = row >> 6
    return ((y * 4 + x) * 4 + z_lo) * 4 + low


def device_at(z, y, x, core):
    return (lax.rem(z, 4), ((y * 4 + x) * 2 + lax.div(z, 4)) * 2 + core)


def aligned(index, multiple):
    return pl.multiple_of(index, multiple)


def comm_kernel(
    limit,
    act_a_hbm, dy_a_hbm, act_e_hbm, dy_e_hbm, w_a_hbm, m_a_hbm, v_a_hbm, w_e_hbm, m_e_hbm, v_e_hbm,
    g_out, f_out, full_a, full_e,
    act_a, dy_a, act_e, dy_e, w_e, m_e, v_e,
    lhs_a, lhs_e, st_a, st_e, pf_a, pf_e,
    cs, cr, own, s1, r1, own2, s2, r2,
    s3_a, s3_e, z3_a, z3_e, r3_a, r3_e,
    n_s, n_r,
    ws_a, ws_e, gr_a, gr_e, g3_a, g3_e,
    send_sem, recv_sem, local_sem,
):
    z_lo = lax.axis_index("expert")
    dp = lax.axis_index("dp")
    core = lax.rem(dp, 2)
    z_hi = lax.rem(lax.div(dp, 2), 2)
    x = lax.rem(lax.div(dp, 4), 4)
    y = lax.div(dp, 16)
    z = z_hi * 4 + z_lo
    other = 1 - core
    peer = device_at(z, y, x, other)

    def zc_mate(dz, dc):
        oz = lax.rem(z + dz, 8)
        oc = core if dc == 0 else other
        return oz, oc

    def plane_mate(dy, dx):
        return device_at(z, lax.rem(y + dy, 4), lax.rem(x + dx, 4), core)

    def axis_mate(axis, d):
        return plane_mate(d, 0) if axis == 0 else plane_mate(0, d)

    place = (y, x)

    kept = []
    waited = []

    def keep(src, dst):
        copy = pltpu.make_async_copy(src, dst, local_sem.at[len(kept)])
        copy.start()
        kept.append(copy)
        return copy

    def need(copies):
        for copy in copies:
            copy.wait()
            waited.append(copy)

    sent = []
    arrived = []

    def send(src, dst, where):
        i = len(sent)
        copy = pltpu.make_async_remote_copy(
            src_ref=src, dst_ref=dst, send_sem=send_sem.at[i], recv_sem=recv_sem.at[i],
            device_id=where, device_id_type=MESH,
        )
        copy.start()
        sent.append(copy)
        return copy

    def arrive(copies):
        for copy in copies:
            copy.wait_recv()
            arrived.append(copy)

    def finish_all():
        arrive([copy for copy in sent if not any(copy is done for done in arrived)])
        for copy in [copy for copy in kept if not any(copy is done for done in waited)]:
            copy.wait()
        for copy in sent:
            copy.wait_send()

    need_act = (keep(act_a_hbm, act_a), keep(act_e_hbm.at[0], act_e))
    need_dy = {}
    for half in range(2):
        for s in range(4):
            cols = pl.ds(aligned((other if half == 0 else core) * HALF + s * SUB, SUB), SUB)
            need_dy[half, s] = (
                keep(dy_a_hbm.at[:, cols], dy_a.at[:, cols]),
                keep(dy_e_hbm.at[0, :, cols], dy_e.at[:, cols]),
            )
    need_state = [
        keep(src, st_a.at[:, pl.ds(k * ROWS, ROWS)]) for k, src in enumerate((w_a_hbm, m_a_hbm, v_a_hbm))
    ] + [keep(src, dst) for src, dst in ((w_e_hbm, w_e), (m_e_hbm, m_e), (v_e_hbm, v_e))]

    barrier = pltpu.get_barrier_semaphore()
    greeted = 0
    for dz in range(8):
        for dc in range(2):
            if dz or dc:
                oz, oc = zc_mate(dz, dc)
                pl.semaphore_signal(barrier, inc=1, device_id=device_at(oz, y, x, oc), device_id_type=MESH)
                greeted += 1
    for dy in range(4):
        for dx in range(4):
            if dy or dx:
                pl.semaphore_signal(barrier, inc=1, device_id=plane_mate(dy, dx), device_id_type=MESH)
                greeted += 1

    r0 = lax.broadcasted_iota(jnp.int32, (256, 256), 0)
    r1_ = lax.broadcasted_iota(jnp.int32, (256, 256), 1)
    pick = jnp.where(r0 == grouped(r1_), 1.0, 0.0).astype(BF16)
    need(need_act)
    lhs_a[...] = lax.dot_general(
        pick, act_a[...], (((1,), (1,)), ((), ())), preferred_element_type=F32
    ).astype(BF16)
    e0 = lax.broadcasted_iota(jnp.int32, (128, 128), 0)
    e1 = lax.broadcasted_iota(jnp.int32, (128, 128), 1)
    same = jnp.where(e0 == e1, 1.0, 0.0).astype(BF16)
    lhs_e[...] = lax.dot_general(
        same, act_e[...], (((1,), (1,)), ((), ())), preferred_element_type=F32
    ).astype(BF16)

    def terms(half, s):
        need(need_dy[half, s])
        cols = pl.ds(aligned((other if half == 0 else core) * HALF + s * SUB, SUB), SUB)
        ga = jnp.dot(lhs_a[...], dy_a[:, cols], preferred_element_type=F32)
        ge = jnp.dot(lhs_e[...], dy_e[:, cols], preferred_element_type=F32)
        return ga.reshape(4, 4, 2, 8, SUB), ge.reshape(4, 4, 8, SUB)

    def piece(ref, part, second, first):
        return ref.at[part, second, first] if part % 2 == 0 else ref.at[part, first, second]

    order = (2, 1, 3, 0)
    copies_c, copies_1 = {}, {}

    def give(s):
        ga, ge = terms(0, s)
        cs[s, :, :, 0:2] = ga.astype(BF16)
        cs[s, :, :, 2] = ge.astype(BF16)
        if s == 0:
            pl.semaphore_wait(barrier, greeted)
        copies_c[s] = send(cs.at[s], cr.at[s], peer)

    def take(s):
        ga, ge = terms(1, s)
        own[s, :, :, 0:2] = ga
        own[s, :, :, 2] = ge
        arrive([copies_c[s]])
        for b in range(4):
            both = own[s, b] + cr[s, b].astype(F32)
            own[s, b] = both
            s1[s, b] = both.astype(BF16)
        first = 1 - s % 2
        if s < 2:
            copies_1[s] = []
            for e in (2, 1, 3):
                to = lax.rem(place[first] + e, 4)
                src = s1.at[s, :, to] if s % 2 == 0 else s1.at[s, to]
                copies_1[s].append(send(src, r1.at[s, e - 1], axis_mate(first, e)))
        else:
            for d in order:
                at = lax.rem(place[s % 2] + d, 4)
                copies_1[s, d] = [
                    send(
                        piece(s1, s, at, lax.rem(place[first] + e, 4)),
                        r1.at[s, e - 1, at],
                        axis_mate(first, e),
                    )
                    for e in (2, 1, 3)
                ]

    give(0)
    z_order = (4, 3, 5, 2, 6, 1, 7, 0)
    my_q = z_lo * 4 + z_hi * 2 + core
    my_e = z_hi * 2 + core
    need(need_state)
    for h in range(2):
        for j in range(2):
            for k, state in enumerate((w_e, m_e, v_e)):
                st_e[h, pl.ds((j * 3 + k) * ROWS, ROWS), :] = state[pl.ds(h * 2 * ROWS + j, ROWS, stride=2), :]
    pf_at_a = pl.ds(aligned(my_q * 3 * ROWS, 8), 3 * ROWS)
    pf_at_e = pl.ds(aligned(my_e * 6 * ROWS, 8), 6 * ROWS)
    copies_pf = []
    for dz in z_order:
        for dc in range(2):
            if dz or dc:
                oz, oc = zc_mate(dz, dc)
                copies_pf.append(send(st_a.at[oc], pf_a.at[pf_at_a], device_at(oz, y, x, oc)))
                if dz in (0, 4):
                    copies_pf.append(send(st_e.at[oc], pf_e.at[pf_at_e], device_at(oz, y, x, oc)))
    pf_a[pf_at_a, :] = st_a[core]
    pf_e[pf_at_e, :] = st_e[core]

    give(1)
    take(0)
    take(1)
    give(2)
    give(3)
    take(2)
    take(3)

    copies_2 = {s: [] for s in range(4)}

    def pass_on(s, d):
        at = lax.rem(place[s % 2] + d, 4)
        total = piece(own, s, at, place[1 - s % 2])[...]
        for e in range(3):
            total = total + r1[s, e, at].astype(F32)
        if d:
            s2[s, d - 1] = total.astype(BF16)
            copies_2[s].append(send(s2.at[s, d - 1], r2.at[s, d - 1], axis_mate(s % 2, d)))
        else:
            own2[s] = total

    for s in (0, 1):
        arrive(copies_1[s])
        for d in order:
            pass_on(s, d)
    for d in order:
        for s in (2, 3):
            arrive(copies_1[s, d])
            pass_on(s, d)

    for s in range(4):
        arrive(copies_2[s])
        total = own2[s]
        for d in range(3):
            total = total + r2[s, d].astype(F32)
        total_a = total[0:2].reshape(16, SUB)
        total_e = total[2]
        for t in range(SROWS):
            lanes = slice(t * LANES, (t + 1) * LANES)
            s3_a[pl.ds(s * SROWS + t, 16, stride=ROWS), :] = total_a[:, lanes]
            s3_e[pl.ds(s * SROWS + t, 8, stride=ROWS), :] = total_e[:, lanes]
    z3_a[...] = s3_a[...].astype(BF16).reshape(16, ROWS, LANES)
    z3_e[...] = s3_e[...].astype(BF16).reshape(4, 2 * ROWS, LANES)

    batch = []
    for dz in z_order:
        for dc in range(2):
            if dz or dc:
                oz, oc = zc_mate(dz, dc)
                q = lax.rem(oz, 4) * 4 + lax.div(oz, 4) * 2 + oc
                batch.append(send(z3_a.at[q], r3_a.at[dc, dz], device_at(oz, y, x, oc)))
                if dz in (0, 4):
                    q = lax.div(oz, 4) * 2 + oc
                    batch.append(send(z3_e.at[q], r3_e.at[dc, dz // 4], device_at(oz, y, x, oc)))
    arrive(batch)

    near = s3_a[pl.ds(aligned(my_q * ROWS, 8), ROWS), :]
    far = r3_a[1, 0].astype(F32)
    for dz in range(1, 8):
        near = near + r3_a[0, dz].astype(F32)
        far = far + r3_a[1, dz].astype(F32)
    near_at = pl.ds(aligned(core * ROWS, 8), ROWS)
    far_at = pl.ds(aligned(other * ROWS, 8), ROWS)
    g_out[0, near_at, :] = near
    g_out[0, far_at, :] = far
    near_e = s3_e[pl.ds(aligned(my_e * 2 * ROWS, 8), 2 * ROWS), :] + r3_e[0, 1].astype(F32)
    far_e = r3_e[1, 0].astype(F32) + r3_e[1, 1].astype(F32)
    for j in range(2):
        g_out[1 + j, near_at, :] = near_e[j * ROWS : (j + 1) * ROWS]
        g_out[1 + j, far_at, :] = far_e[j * ROWS : (j + 1) * ROWS]

    square = jnp.zeros((8, LANES), F32)
    for piece in (near, far, near_e, far_e):
        for i in range(piece.shape[0] // 8):
            part_of = piece[i * 8 : (i + 1) * 8]
            square = square + part_of * part_of
    n_s[0] = square
    batch = []
    for dz in z_order:
        for dc in range(2):
            if dz or dc:
                oz, oc = zc_mate(dz, dc)
                batch.append(send(n_s.at[0], n_r.at[0, dz * 2 + dc], device_at(oz, y, x, oc)))
    ws_a[core] = near.astype(BF16)
    ws_a[other] = far.astype(BF16)
    ws_e[core] = near_e.astype(BF16)
    ws_e[other] = far_e.astype(BF16)
    copies_g = []
    for dz in z_order:
        for dc in range(2):
            if dz or dc:
                oz, oc = zc_mate(dz, dc)
                copies_g.append(send(ws_a.at[oc], gr_a.at[my_q], device_at(oz, y, x, oc)))
                if dz in (0, 4):
                    copies_g.append(send(ws_e.at[oc], gr_e.at[my_e], device_at(oz, y, x, oc)))
    gr_a[my_q] = ws_a[core]
    gr_e[my_e] = ws_e[core]
    arrive(batch)
    for i in range(1, 16):
        square = square + n_r[0, i]
    n_s[1] = square
    batch = []
    for dy in order:
        for dx in order:
            if dy or dx:
                batch.append(send(n_s.at[1], n_r.at[1, dy * 4 + dx], plane_mate(dy, dx)))
    arrive(copies_g)
    g3_a[...] = gr_a[...].astype(F32).reshape(16 * ROWS, LANES)
    g3_e[...] = gr_e[...].astype(F32).reshape(8 * ROWS, LANES)
    arrive(copies_pf)
    arrive(batch)
    for i in range(1, 16):
        square = square + n_r[1, i]
    norm = jnp.sqrt(jnp.sum(square, keepdims=True))
    factor = jnp.minimum(1.0, limit / (norm + 1e-06))
    f_out[...] = jnp.broadcast_to(factor, (8, LANES))

    def new_tile(rows, grad, state, t):
        values = [state[pl.ds(k * ROWS + t, rows, stride=3 * ROWS), :] for k in range(3)]
        return adamw(grad[pl.ds(t, rows, stride=ROWS), :], *values, factor)[0].astype(BF16)

    even = 2 * lax.rem(lax.div(z_lo + 1, 2), 2)
    odd = 2 * lax.div(z_lo, 2) + 1
    mine = (even, odd)
    swapped = (2 - even, 4 - odd)
    swap_z = (lax.rem(z + 1 + 6 * lax.rem(z, 2), 8), lax.rem(z + 7 - 6 * lax.rem(z, 2), 8))

    def spread(ref, lead, part, at):
        here = block(ref, lead, part, at, place[1 - part])
        return [send(here, here, axis_mate(1 - part, e)) for e in (2, 1, 3)]

    def block(ref, lead, part, second, first):
        return ref.at[lead, second, first] if part == 0 else ref.at[lead, first, second]

    def strip(ref, lead, part, second):
        return ref.at[lead, second] if part == 0 else ref.at[lead, :, second]

    def deliver(ref, lead, part, second):
        src = strip(ref, lead, part, second)
        send(src, src, peer)

    gt_a = full_a.at[core]
    gt_e = full_e.at[core]
    first_a, second_a, first_e, second_e = {}, {}, {}, {}
    for part in range(2):
        for t in range(SROWS):
            tile = new_tile(16, g3_a, pf_a, mine[part] * SROWS + t)
            gt_a[mine[part], y, x, :, :, pl.ds(t * LANES, LANES)] = tile.reshape(2, 8, LANES)
        here = gt_a.at[mine[part], y, x]
        for d in (2, 1, 3):
            second_a[part, d] = send(here, here, axis_mate(part, d))
        first_a[part, 0] = spread(gt_a, mine[part], part, place[part])
    for part in range(2):
        for t in range(PROWS):
            gt_e[part, y, x, :, pl.ds(t * LANES, LANES)] = new_tile(8, g3_e, pf_e, part * PROWS + t)
        here = gt_e.at[part, y, x]
        for d in (2, 1, 3):
            second_e[part, d] = send(here, here, axis_mate(part, d))
        first_e[part, 0] = spread(gt_e, part, part, place[part])

    def from_mate(part, d):
        return lax.rem(place[part] + 4 - d, 4)

    for d in (1, 3, 2):
        for part in range(2):
            arrive([second_a[part, d]])
            first_a[part, d] = spread(gt_a, mine[part], part, from_mate(part, d))
    for d in (1, 3, 2):
        for part in range(2):
            arrive([second_e[part, d]])
            first_e[part, d] = spread(gt_e, part, part, from_mate(part, d))
    swaps = {}
    for d in (0, 1, 3, 2):
        for part in range(2):
            at = from_mate(part, d)
            arrive(first_a[part, d])
            ready = strip(gt_a, mine[part], part, at)
            swaps[part, d] = send(ready, ready, device_at(swap_z[part], y, x, core))
            deliver(gt_a, mine[part], part, at)
    for d in (0, 1, 3, 2):
        for part in range(2):
            at = from_mate(part, d)
            arrive(first_e[part, d])
            deliver(gt_e, part, part, at)
            arrive([swaps[part, d]])
            deliver(gt_a, swapped[part], part, at)
    finish_all()


def finish_kernel(
    full_a, full_e, g, f, w_a, m_a, v_a, w_e, m_e, v_e,
    wa_o, ma_o, va_o, we_o, me_o, ve_o, attn_o, exp_o,
    attn, new_a, new_e, pick, out_sem,
):
    r0 = lax.broadcasted_iota(jnp.int32, (256, 256), 0)
    r1 = lax.broadcasted_iota(jnp.int32, (256, 256), 1)
    pick[...] = jnp.where(grouped(r0) == r1, 1.0, 0.0).astype(BF16)

    writes = []

    def write(src, dst):
        copy = pltpu.make_async_copy(src, dst, out_sem.at[len(writes)])
        copy.start()
        writes.append(copy)

    for i in range(2 * HALF // PART):
        write(full_e.at[i], exp_o.at[:, :, pl.ds(i * PART, PART)])
    for i in range(2 * HALF // SUB):
        gathered = full_a[i].reshape(256, SUB)
        attn[i] = jnp.dot(pick[...], gathered, preferred_element_type=F32).astype(BF16)
        write(attn.at[i], attn_o.at[:, pl.ds(i * SUB, SUB)])
    factor = f[0:1, 0:1]
    new = adamw(g[0], w_a[...], m_a[...], v_a[...], factor)
    for k, ref in enumerate((wa_o, ma_o, va_o)):
        new_a[k] = new[k]
        write(new_a.at[k], ref)
    for j in range(2):
        rows = pl.ds(j, 2 * ROWS, stride=2)
        new = adamw(g[1 + j], w_e[rows, :], m_e[rows, :], v_e[rows, :], factor)
        for k in range(3):
            new_e[k, rows, :] = new[k]
    for k, ref in enumerate((we_o, me_o, ve_o)):
        write(new_e.at[k], ref)
    for copy in writes:
        copy.wait()


def comm_part(act_attn, dy_attn, act_exp, dy_exp, w_attn, m_attn, v_attn, w_exp, m_exp, v_exp):
    width = w_attn.shape[1]
    total_params = width * (act_attn.shape[1] + lax.axis_size("expert") * act_exp.shape[2])
    limit = 0.5 * math.sqrt(total_params)
    attn_state = [v.reshape(2, ROWS, LANES) for v in (w_attn, m_attn, v_attn)]
    exp_state = [
        v.reshape(2, 2 * ROWS, LANES).transpose(1, 0, 2).reshape(4 * ROWS, LANES)
        for v in (w_exp, m_exp, v_exp)
    ]
    hbm = pl.BlockSpec(memory_space=pltpu.HBM)
    vmem = pl.BlockSpec(memory_space=pltpu.VMEM)
    n_send = 230

    def blocks(dtype, *lead):
        return pltpu.VMEM(lead + (3, 8, SUB), dtype)

    outs = pl.pallas_call(
        lambda *refs: comm_kernel(limit, *refs),
        out_shape=(
            jax.ShapeDtypeStruct((3, 2 * ROWS, LANES), F32),
            jax.ShapeDtypeStruct((8, LANES), F32),
            jax.ShapeDtypeStruct((2, 4, 4, 4, 2, 8, SUB), BF16),
            jax.ShapeDtypeStruct((2, 2, 4, 4, 8, PART), BF16),
        ),
        in_specs=[hbm] * 10,
        out_specs=(vmem,) * 4,
        scratch_shapes=[
            pltpu.VMEM((256, 256), BF16),
            pltpu.VMEM((256, 4 * PART), BF16),
            pltpu.VMEM((128, 128), BF16),
            pltpu.VMEM((128, 4 * PART), BF16),
            *[pltpu.VMEM((4 * ROWS, LANES), F32)] * 3,
            pltpu.VMEM((256, 256), BF16),
            pltpu.VMEM((128, 128), BF16),
            pltpu.VMEM((2, 3 * ROWS, LANES), F32),
            pltpu.VMEM((2, 6 * ROWS, LANES), F32),
            pltpu.VMEM((16 * 3 * ROWS, LANES), F32),
            pltpu.VMEM((8 * 3 * ROWS, LANES), F32),
            blocks(BF16, 4, 4, 4),
            blocks(BF16, 4, 4, 4),
            blocks(F32, 4, 4, 4),
            blocks(BF16, 4, 4, 4),
            blocks(BF16, 4, 3, 4),
            blocks(F32, 4),
            blocks(BF16, 4, 3),
            blocks(BF16, 4, 3),
            pltpu.VMEM((16 * ROWS, LANES), F32),
            pltpu.VMEM((8 * ROWS, LANES), F32),
            pltpu.VMEM((16, ROWS, LANES), BF16),
            pltpu.VMEM((4, 2 * ROWS, LANES), BF16),
            pltpu.VMEM((2, 8, ROWS, LANES), BF16),
            pltpu.VMEM((2, 2, 2 * ROWS, LANES), BF16),
            pltpu.VMEM((2, 8, LANES), F32),
            pltpu.VMEM((2, 16, 8, LANES), F32),
            pltpu.VMEM((2, ROWS, LANES), BF16),
            pltpu.VMEM((2, 2 * ROWS, LANES), BF16),
            pltpu.VMEM((16, ROWS, LANES), BF16),
            pltpu.VMEM((4, 2 * ROWS, LANES), BF16),
            pltpu.VMEM((16 * ROWS, LANES), F32),
            pltpu.VMEM((8 * ROWS, LANES), F32),
            pltpu.SemaphoreType.DMA((n_send,)),
            pltpu.SemaphoreType.DMA((n_send,)),
            pltpu.SemaphoreType.DMA((80,)),
        ],
        compiler_params=pltpu.CompilerParams(
            collective_id=0, has_side_effects=True, vmem_limit_bytes=36 * 1024 * 1024
        ),
    )(*[pltpu.with_memory_space_constraint(v, pltpu.HBM) for v in (act_attn, dy_attn, act_exp, dy_exp, *attn_state, *exp_state)])
    return outs, attn_state, exp_state


def body(act_attn, dy_attn, act_exp, dy_exp, *state):
    width = dy_attn.shape[1]
    (g, f, full_a, full_e), attn_state, exp_state = comm_part(act_attn, dy_attn, act_exp, dy_exp, *state)
    a_shape, e_shape = (2 * ROWS, LANES), (4 * ROWS, LANES)
    steps = width // SUB
    hbm = pl.BlockSpec(memory_space=pltpu.HBM)
    vmem = pl.BlockSpec(memory_space=pltpu.VMEM)
    outs = pl.pallas_call(
        finish_kernel,
        out_shape=(
            *[jax.ShapeDtypeStruct(a_shape, F32)] * 3,
            *[jax.ShapeDtypeStruct(e_shape, F32)] * 3,
            jax.ShapeDtypeStruct((256, width), BF16),
            jax.ShapeDtypeStruct((16, 8, width), BF16),
        ),
        in_specs=[vmem] * 10,
        out_specs=(hbm,) * 8,
        scratch_shapes=[
            pltpu.VMEM((steps, 256, SUB), BF16),
            pltpu.VMEM((3,) + a_shape, F32),
            pltpu.VMEM((3,) + e_shape, F32),
            pltpu.VMEM((256, 256), BF16),
            pltpu.SemaphoreType.DMA((2 * steps + 6,)),
        ],
        compiler_params=pltpu.CompilerParams(vmem_limit_bytes=16 * 1024 * 1024),
    )(full_a.reshape(steps, 16, 2, 8, SUB), full_e.reshape(steps // 2, 16, 8, PART), g, f, *[v.reshape(a_shape) for v in attn_state], *exp_state)
    attn_new = [v.reshape(1, width) for v in outs[:3]]
    exp_new = [
        v.reshape(2 * ROWS, 2, LANES).transpose(1, 0, 2).reshape(1, 2, width) for v in outs[3:6]
    ]
    return (*attn_new, *exp_new, outs[6], outs[7].reshape(1, 128, width))


def solution(mesh):
    rows = P(("expert", "dp"), None)
    owned = P("expert", "dp", None)
    return jax.shard_map(
        body,
        mesh=mesh,
        in_specs=(rows, rows, owned, owned, rows, rows, rows, owned, owned, owned),
        out_specs=(rows, rows, rows, owned, owned, owned, P(), P("expert", None, None)),
        check_vma=False,
    )
```

```python
import math

import jax
import jax.numpy as jnp
from jax import lax
from jax.experimental import pallas as pl
from jax.experimental.pallas import tpu as pltpu
from jax.sharding import PartitionSpec as P

beta_first = 0.9
beta_second = 0.95
bias_first = 1.0 - 0.9**10
bias_second = 1.0 - 0.95**10
learn_rate = 0.01
decay_rate = 0.1
adam_eps = 1e-08

MESH = pl.DeviceIdType.MESH
F32 = jnp.float32
BF16 = jnp.bfloat16
HALF = 3072
PART = 1536
LANES = 128
ROWS = HALF // LANES
PROWS = PART // LANES
SUB = 768
SROWS = SUB // LANES


def adamw(grad, weight, moment, second, factor):
    scaled = factor * grad
    moment_new = beta_first * moment + (1.0 - beta_first) * scaled
    second_new = beta_second * second + (1.0 - beta_second) * scaled * scaled
    update = moment_new / bias_first / (jnp.sqrt(second_new / bias_second) + adam_eps)
    weight_new = weight - learn_rate * (update + decay_rate * weight)
    return (weight_new, moment_new, second_new)


def grouped(row):
    low = row & 3
    x = (row >> 2) & 3
    y = (row >> 4) & 3
    z_lo = row >> 6
    return ((y * 4 + x) * 4 + z_lo) * 4 + low


def device_at(z, y, x, core):
    return (z & 3, y * 16 + x * 4 + (z >> 2) * 2 + core)


def aligned(index, multiple):
    return pl.multiple_of(index, multiple)


def comm_kernel(
    limit,
    act_a_hbm, dy_a_hbm, act_e_hbm, dy_e_hbm, w_a_hbm, m_a_hbm, v_a_hbm, w_e_hbm, m_e_hbm, v_e_hbm,
    g_out, f_out, full_a, full_e,
    act_a, dy_a, act_e, dy_e, w_e, m_e, v_e,
    lhs_a, lhs_e, st_a, st_e, pf_a, pf_e,
    cs, cr, own, s1, r1, own2, s2, r2,
    s3_a, s3_e, z3_a, z3_e, r3_a, r3_e,
    n_s, n_r,
    ws_a, ws_e, gr_a, gr_e, g3_a, g3_e,
    send_sem, recv_sem, local_sem,
):
    z_lo = lax.axis_index("expert")
    dp = lax.axis_index("dp")
    core = dp & 1
    z_hi = (dp >> 1) & 1
    x = (dp >> 2) & 3
    y = dp >> 4
    z = z_hi * 4 + z_lo
    other = 1 - core
    peer = device_at(z, y, x, other)

    zc_places, zc_devices, plane_devices = {}, {}, {}
    for dz in range(8):
        for dc in range(2):
            oz, oc = (z + dz) & 7, core if dc == 0 else other
            zc_places[dz, dc] = (oz, oc)
            zc_devices[dz, dc] = device_at(oz, y, x, oc)
    for dy in range(4):
        for dx in range(4):
            plane_devices[dy, dx] = device_at(z, (y + dy) & 3, (x + dx) & 3, core)

    def plane_mate(dy, dx):
        return plane_devices[dy, dx]

    def axis_mate(axis, d):
        return plane_mate(d, 0) if axis == 0 else plane_mate(0, d)

    place = (y, x)

    kept = []
    waited = []

    def keep(src, dst):
        copy = pltpu.make_async_copy(src, dst, local_sem.at[len(kept)])
        copy.start()
        kept.append(copy)
        return copy

    def need(copies):
        for copy in copies:
            copy.wait()
            waited.append(copy)

    sent = []
    arrived = []

    def send(src, dst, where):
        i = len(sent)
        copy = pltpu.make_async_remote_copy(
            src_ref=src, dst_ref=dst, send_sem=send_sem.at[i], recv_sem=recv_sem.at[i],
            device_id=where, device_id_type=MESH,
        )
        copy.start()
        sent.append(copy)
        return copy

    def arrive(copies):
        for copy in copies:
            copy.wait_recv()
            arrived.append(copy)

    def finish_all():
        arrive([copy for copy in sent if not any(copy is done for done in arrived)])
        for copy in [copy for copy in kept if not any(copy is done for done in waited)]:
            copy.wait()
        for copy in sent:
            copy.wait_send()

    need_act = (keep(act_a_hbm, act_a), keep(act_e_hbm.at[0], act_e))
    barrier = pltpu.get_barrier_semaphore()
    greeted = 0
    for dz in range(8):
        for dc in range(2):
            if dz or dc:
                oz, oc = zc_places[dz, dc]
                pl.semaphore_signal(barrier, inc=1, device_id=zc_devices[dz, dc], device_id_type=MESH)
                greeted += 1
    for dy in range(4):
        for dx in range(4):
            if dy or dx:
                pl.semaphore_signal(barrier, inc=1, device_id=plane_mate(dy, dx), device_id_type=MESH)
                greeted += 1

    need_dy = {}
    for half in range(2):
        for s in range(4):
            cols = pl.ds(aligned((other if half == 0 else core) * HALF + s * SUB, SUB), SUB)
            need_dy[half, s] = (
                keep(dy_a_hbm.at[:, cols], dy_a.at[:, cols]),
                keep(dy_e_hbm.at[0, :, cols], dy_e.at[:, cols]),
            )
    need_state = [
        keep(src, st_a.at[:, pl.ds(k * ROWS, ROWS)]) for k, src in enumerate((w_a_hbm, m_a_hbm, v_a_hbm))
    ] + [keep(src, dst) for src, dst in ((w_e_hbm, w_e), (m_e_hbm, m_e), (v_e_hbm, v_e))]

    r0 = lax.broadcasted_iota(jnp.int32, (256, 256), 0)
    r1_ = lax.broadcasted_iota(jnp.int32, (256, 256), 1)
    pick = jnp.where(r0 == grouped(r1_), 1.0, 0.0).astype(BF16)
    need(need_act)
    lhs_a[...] = lax.dot_general(
        pick, act_a[...], (((1,), (1,)), ((), ())), preferred_element_type=F32
    ).astype(BF16)
    e0 = lax.broadcasted_iota(jnp.int32, (128, 128), 0)
    e1 = lax.broadcasted_iota(jnp.int32, (128, 128), 1)
    same = jnp.where(e0 == e1, 1.0, 0.0).astype(BF16)
    lhs_e[...] = lax.dot_general(
        same, act_e[...], (((1,), (1,)), ((), ())), preferred_element_type=F32
    ).astype(BF16)

    def terms(half, s):
        need(need_dy[half, s])
        cols = pl.ds(aligned((other if half == 0 else core) * HALF + s * SUB, SUB), SUB)
        ga = jnp.dot(lhs_a[...], dy_a[:, cols], preferred_element_type=F32)
        ge = jnp.dot(lhs_e[...], dy_e[:, cols], preferred_element_type=F32)
        return ga.reshape(4, 4, 2, 8, SUB), ge.reshape(4, 4, 8, SUB)

    def piece(ref, part, second, first):
        return ref.at[part, second, first] if part % 2 == 0 else ref.at[part, first, second]

    order = (2, 1, 3, 0)
    copies_c, copies_1 = {}, {}

    def give(s):
        ga, ge = terms(0, s)
        cs[s, :, :, 0:2] = ga.astype(BF16)
        cs[s, :, :, 2] = ge.astype(BF16)
        if s == 0:
            pl.semaphore_wait(barrier, greeted)
        copies_c[s] = send(cs.at[s], cr.at[s], peer)

    def take(s):
        ga, ge = terms(1, s)
        own[s, :, :, 0:2] = ga
        own[s, :, :, 2] = ge
        arrive([copies_c[s]])
        for b in range(4):
            both = own[s, b] + cr[s, b].astype(F32)
            own[s, b] = both
            s1[s, b] = both.astype(BF16)
        first = 1 - s % 2
        if s < 2:
            copies_1[s] = []
            for e in (2, 1, 3):
                to = ((place[first] + e) & 3)
                src = s1.at[s, :, to] if s % 2 == 0 else s1.at[s, to]
                copies_1[s].append(send(src, r1.at[s, e - 1], axis_mate(first, e)))
        else:
            for d in order:
                at = ((place[s % 2] + d) & 3)
                copies_1[s, d] = [
                    send(
                        piece(s1, s, at, ((place[first] + e) & 3)),
                        r1.at[s, e - 1, at],
                        axis_mate(first, e),
                    )
                    for e in (2, 1, 3)
                ]

    give(0)
    z_order = (4, 3, 5, 2, 6, 1, 7, 0)
    my_q = z_lo * 4 + z_hi * 2 + core
    my_e = z_hi * 2 + core
    need(need_state)
    for h in range(2):
        for j in range(2):
            for k, state in enumerate((w_e, m_e, v_e)):
                st_e[h, pl.ds((j * 3 + k) * ROWS, ROWS), :] = state[pl.ds(h * 2 * ROWS + j, ROWS, stride=2), :]
    pf_at_a = pl.ds(aligned(my_q * 3 * ROWS, 8), 3 * ROWS)
    pf_at_e = pl.ds(aligned(my_e * 6 * ROWS, 8), 6 * ROWS)
    copies_pf = []
    for dz in z_order:
        for dc in range(2):
            if dz or dc:
                oz, oc = zc_places[dz, dc]
                copies_pf.append(send(st_a.at[oc], pf_a.at[pf_at_a], zc_devices[dz, dc]))
                if dz in (0, 4):
                    copies_pf.append(send(st_e.at[oc], pf_e.at[pf_at_e], zc_devices[dz, dc]))
    pf_a[pf_at_a, :] = st_a[core]
    pf_e[pf_at_e, :] = st_e[core]

    give(1)
    take(0)
    take(1)
    give(2)
    give(3)
    take(2)
    take(3)

    copies_2 = {s: [] for s in range(4)}

    def pass_on(s, d):
        at = ((place[s % 2] + d) & 3)
        total = piece(own, s, at, place[1 - s % 2])[...]
        for e in range(3):
            total = total + r1[s, e, at].astype(F32)
        if d:
            s2[s, d - 1] = total.astype(BF16)
            copies_2[s].append(send(s2.at[s, d - 1], r2.at[s, d - 1], axis_mate(s % 2, d)))
        else:
            own2[s] = total

    for s in (0, 1):
        arrive(copies_1[s])
        for d in order:
            pass_on(s, d)
    for d in order:
        for s in (2, 3):
            arrive(copies_1[s, d])
            pass_on(s, d)

    for s in range(4):
        arrive(copies_2[s])
        total = own2[s]
        for d in range(3):
            total = total + r2[s, d].astype(F32)
        total_a = total[0:2].reshape(16, SUB)
        total_e = total[2]
        for t in range(SROWS):
            lanes = slice(t * LANES, (t + 1) * LANES)
            s3_a[pl.ds(s * SROWS + t, 16, stride=ROWS), :] = total_a[:, lanes]
            s3_e[pl.ds(s * SROWS + t, 8, stride=ROWS), :] = total_e[:, lanes]
    z3_a[...] = s3_a[...].astype(BF16).reshape(16, ROWS, LANES)
    z3_e[...] = s3_e[...].astype(BF16).reshape(4, 2 * ROWS, LANES)

    batch = []
    for dz in z_order:
        for dc in range(2):
            if dz or dc:
                oz, oc = zc_places[dz, dc]
                q = (oz & 3) * 4 + (oz >> 2) * 2 + oc
                batch.append(send(z3_a.at[q], r3_a.at[dc, dz], zc_devices[dz, dc]))
                if dz in (0, 4):
                    q = (oz >> 2) * 2 + oc
                    batch.append(send(z3_e.at[q], r3_e.at[dc, dz // 4], zc_devices[dz, dc]))
    arrive(batch)

    near = s3_a[pl.ds(aligned(my_q * ROWS, 8), ROWS), :]
    far = r3_a[1, 0].astype(F32)
    for dz in range(1, 8):
        near = near + r3_a[0, dz].astype(F32)
        far = far + r3_a[1, dz].astype(F32)
    near_at = pl.ds(aligned(core * ROWS, 8), ROWS)
    far_at = pl.ds(aligned(other * ROWS, 8), ROWS)
    g_out[0, near_at, :] = near
    g_out[0, far_at, :] = far
    near_e = s3_e[pl.ds(aligned(my_e * 2 * ROWS, 8), 2 * ROWS), :] + r3_e[0, 1].astype(F32)
    far_e = r3_e[1, 0].astype(F32) + r3_e[1, 1].astype(F32)
    for j in range(2):
        g_out[1 + j, near_at, :] = near_e[j * ROWS : (j + 1) * ROWS]
        g_out[1 + j, far_at, :] = far_e[j * ROWS : (j + 1) * ROWS]

    square = jnp.zeros((8, LANES), F32)
    for piece in (near, far, near_e, far_e):
        for i in range(piece.shape[0] // 8):
            part_of = piece[i * 8 : (i + 1) * 8]
            square = square + part_of * part_of
    n_s[0] = square
    batch = []
    for dz in z_order:
        for dc in range(2):
            if dz or dc:
                oz, oc = zc_places[dz, dc]
                batch.append(send(n_s.at[0], n_r.at[0, dz * 2 + dc], zc_devices[dz, dc]))
    ws_a[core] = near.astype(BF16)
    ws_a[other] = far.astype(BF16)
    ws_e[core] = near_e.astype(BF16)
    ws_e[other] = far_e.astype(BF16)
    copies_g = []
    for dz in z_order:
        for dc in range(2):
            if dz or dc:
                oz, oc = zc_places[dz, dc]
                copies_g.append(send(ws_a.at[oc], gr_a.at[my_q], zc_devices[dz, dc]))
                if dz in (0, 4):
                    copies_g.append(send(ws_e.at[oc], gr_e.at[my_e], zc_devices[dz, dc]))
    gr_a[my_q] = ws_a[core]
    gr_e[my_e] = ws_e[core]
    arrive(batch)
    for i in range(1, 16):
        square = square + n_r[0, i]
    n_s[1] = square
    batch = []
    for dy in order:
        for dx in order:
            if dy or dx:
                batch.append(send(n_s.at[1], n_r.at[1, dy * 4 + dx], plane_mate(dy, dx)))
    arrive(copies_g)
    g3_a[...] = gr_a[...].astype(F32).reshape(16 * ROWS, LANES)
    g3_e[...] = gr_e[...].astype(F32).reshape(8 * ROWS, LANES)
    arrive(copies_pf)
    arrive(batch)
    for i in range(1, 16):
        square = square + n_r[1, i]
    norm = jnp.sqrt(jnp.sum(square, keepdims=True))
    factor = jnp.minimum(1.0, limit / (norm + 1e-06))
    f_out[...] = jnp.broadcast_to(factor, (8, LANES))

    def new_tile(rows, grad, state, t):
        values = [state[pl.ds(k * ROWS + t, rows, stride=3 * ROWS), :] for k in range(3)]
        return adamw(grad[pl.ds(t, rows, stride=ROWS), :], *values, factor)[0].astype(BF16)

    even = ((z_lo + 1) & 2)
    odd = (z_lo & 2) + 1
    mine = (even, odd)
    swapped = (2 - even, 4 - odd)
    swap_z = (z + 1 - 2 * (z & 1), (z + 7 + 2 * (z & 1)) & 7)

    def spread(ref, lead, part, at):
        here = block(ref, lead, part, at, place[1 - part])
        return [send(here, here, axis_mate(1 - part, e)) for e in (2, 1, 3)]

    def block(ref, lead, part, second, first):
        return ref.at[lead, second, first] if part == 0 else ref.at[lead, first, second]

    def strip(ref, lead, part, second):
        return ref.at[lead, second] if part == 0 else ref.at[lead, :, second]

    def deliver(ref, lead, part, second):
        src = strip(ref, lead, part, second)
        send(src, src, peer)

    gt_a = full_a.at[core]
    gt_e = full_e.at[core]
    first_a, second_a, first_e, second_e = {}, {}, {}, {}
    for part in range(2):
        for t in range(SROWS):
            tile = new_tile(16, g3_a, pf_a, mine[part] * SROWS + t)
            gt_a[mine[part], y, x, :, :, pl.ds(t * LANES, LANES)] = tile.reshape(2, 8, LANES)
        here = gt_a.at[mine[part], y, x]
        for d in (2, 1, 3):
            second_a[part, d] = send(here, here, axis_mate(part, d))
        first_a[part, 0] = spread(gt_a, mine[part], part, place[part])
    for part in range(2):
        for t in range(PROWS):
            gt_e[part, y, x, :, pl.ds(t * LANES, LANES)] = new_tile(8, g3_e, pf_e, part * PROWS + t)
        here = gt_e.at[part, y, x]
        for d in (2, 1, 3):
            second_e[part, d] = send(here, here, axis_mate(part, d))

    def from_mate(part, d):
        return ((place[part] + 4 - d) & 3)

    for d in (1, 3, 2):
        for part in range(2):
            arrive([second_a[part, d]])
            first_a[part, d] = spread(gt_a, mine[part], part, from_mate(part, d))
    for part in range(2):
        arrive([second_e[part, d] for d in (1, 3, 2)])
        for e in (2, 1, 3):
            here = gt_e.at[0, :, x] if part == 0 else gt_e.at[1, y]
            first_e[part, e] = send(here, here, axis_mate(1 - part, e))
    swaps = {}

    def pass_attention(d):
        for part in range(2):
            at = from_mate(part, d)
            arrive(first_a[part, d])
            ready = strip(gt_a, mine[part], part, at)
            swaps[part, d] = send(ready, ready, device_at(swap_z[part], y, x, core))
            deliver(gt_a, mine[part], part, at)

    def end_expert(e):
        for part in range(2):
            if e:
                arrive([first_e[part, e]])
            at = (place[1 - part] + 4 - e) & 3
            src = gt_e.at[0, :, at] if part == 0 else gt_e.at[1, at]
            send(src, src, peer)

    def end_swap(d):
        for part in range(2):
            arrive([swaps[part, d]])
            deliver(gt_a, swapped[part], part, from_mate(part, d))

    pass_attention(0)
    pass_attention(1)
    end_expert(0)
    pass_attention(3)
    end_swap(0)
    pass_attention(2)
    end_expert(1)
    end_swap(1)
    end_expert(3)
    end_swap(3)
    end_expert(2)
    end_swap(2)
    finish_all()


def finish_kernel(
    full_a, full_e, g, f, w_a, m_a, v_a, w_e, m_e, v_e,
    wa_o, ma_o, va_o, we_o, me_o, ve_o, attn_o, exp_o,
    attn, new_a, new_e, pick, out_sem,
):
    r0 = lax.broadcasted_iota(jnp.int32, (256, 256), 0)
    r1 = lax.broadcasted_iota(jnp.int32, (256, 256), 1)
    pick[...] = jnp.where(grouped(r0) == r1, 1.0, 0.0).astype(BF16)

    writes = []

    def write(src, dst):
        copy = pltpu.make_async_copy(src, dst, out_sem.at[len(writes)])
        copy.start()
        writes.append(copy)

    for i in range(2 * HALF // PART):
        write(full_e.at[i], exp_o.at[:, :, pl.ds(i * PART, PART)])
    for i in range(2 * HALF // SUB):
        gathered = full_a[i].reshape(256, SUB)
        attn[i] = jnp.dot(pick[...], gathered, preferred_element_type=F32).astype(BF16)
        write(attn.at[i], attn_o.at[:, pl.ds(i * SUB, SUB)])
    factor = f[0:1, 0:1]
    new = adamw(g[0], w_a[...], m_a[...], v_a[...], factor)
    for k, ref in enumerate((wa_o, ma_o, va_o)):
        new_a[k] = new[k]
        write(new_a.at[k], ref)
    for j in range(2):
        rows = pl.ds(j, 2 * ROWS, stride=2)
        new = adamw(g[1 + j], w_e[rows, :], m_e[rows, :], v_e[rows, :], factor)
        for k in range(3):
            new_e[k, rows, :] = new[k]
    for k, ref in enumerate((we_o, me_o, ve_o)):
        write(new_e.at[k], ref)
    for copy in writes:
        copy.wait()


def comm_part(act_attn, dy_attn, act_exp, dy_exp, w_attn, m_attn, v_attn, w_exp, m_exp, v_exp):
    width = w_attn.shape[1]
    total_params = width * (act_attn.shape[1] + lax.axis_size("expert") * act_exp.shape[2])
    limit = 0.5 * math.sqrt(total_params)
    attn_state = [v.reshape(2, ROWS, LANES) for v in (w_attn, m_attn, v_attn)]
    exp_state = [
        v.reshape(2, 2 * ROWS, LANES).transpose(1, 0, 2).reshape(4 * ROWS, LANES)
        for v in (w_exp, m_exp, v_exp)
    ]
    hbm = pl.BlockSpec(memory_space=pltpu.HBM)
    vmem = pl.BlockSpec(memory_space=pltpu.VMEM)
    n_send = 230

    def blocks(dtype, *lead):
        return pltpu.VMEM(lead + (3, 8, SUB), dtype)

    outs = pl.pallas_call(
        lambda *refs: comm_kernel(limit, *refs),
        out_shape=(
            jax.ShapeDtypeStruct((3, 2 * ROWS, LANES), F32),
            jax.ShapeDtypeStruct((8, LANES), F32),
            jax.ShapeDtypeStruct((2, 4, 4, 4, 2, 8, SUB), BF16),
            jax.ShapeDtypeStruct((2, 2, 4, 4, 8, PART), BF16),
        ),
        in_specs=[hbm] * 10,
        out_specs=(vmem,) * 4,
        scratch_shapes=[
            pltpu.VMEM((256, 256), BF16),
            pltpu.VMEM((256, 4 * PART), BF16),
            pltpu.VMEM((128, 128), BF16),
            pltpu.VMEM((128, 4 * PART), BF16),
            *[pltpu.VMEM((4 * ROWS, LANES), F32)] * 3,
            pltpu.VMEM((256, 256), BF16),
            pltpu.VMEM((128, 128), BF16),
            pltpu.VMEM((2, 3 * ROWS, LANES), F32),
            pltpu.VMEM((2, 6 * ROWS, LANES), F32),
            pltpu.VMEM((16 * 3 * ROWS, LANES), F32),
            pltpu.VMEM((8 * 3 * ROWS, LANES), F32),
            blocks(BF16, 4, 4, 4),
            blocks(BF16, 4, 4, 4),
            blocks(F32, 4, 4, 4),
            blocks(BF16, 4, 4, 4),
            blocks(BF16, 4, 3, 4),
            blocks(F32, 4),
            blocks(BF16, 4, 3),
            blocks(BF16, 4, 3),
            pltpu.VMEM((16 * ROWS, LANES), F32),
            pltpu.VMEM((8 * ROWS, LANES), F32),
            pltpu.VMEM((16, ROWS, LANES), BF16),
            pltpu.VMEM((4, 2 * ROWS, LANES), BF16),
            pltpu.VMEM((2, 8, ROWS, LANES), BF16),
            pltpu.VMEM((2, 2, 2 * ROWS, LANES), BF16),
            pltpu.VMEM((2, 8, LANES), F32),
            pltpu.VMEM((2, 16, 8, LANES), F32),
            pltpu.VMEM((2, ROWS, LANES), BF16),
            pltpu.VMEM((2, 2 * ROWS, LANES), BF16),
            pltpu.VMEM((16, ROWS, LANES), BF16),
            pltpu.VMEM((4, 2 * ROWS, LANES), BF16),
            pltpu.VMEM((16 * ROWS, LANES), F32),
            pltpu.VMEM((8 * ROWS, LANES), F32),
            pltpu.SemaphoreType.DMA((n_send,)),
            pltpu.SemaphoreType.DMA((n_send,)),
            pltpu.SemaphoreType.DMA((80,)),
        ],
        compiler_params=pltpu.CompilerParams(
            collective_id=0, has_side_effects=True, vmem_limit_bytes=36 * 1024 * 1024
        ),
    )(*[pltpu.with_memory_space_constraint(v, pltpu.HBM) for v in (act_attn, dy_attn, act_exp, dy_exp, *attn_state, *exp_state)])
    return outs, attn_state, exp_state


def body(act_attn, dy_attn, act_exp, dy_exp, *state):
    width = dy_attn.shape[1]
    (g, f, full_a, full_e), attn_state, exp_state = comm_part(act_attn, dy_attn, act_exp, dy_exp, *state)
    a_shape, e_shape = (2 * ROWS, LANES), (4 * ROWS, LANES)
    steps = width // SUB
    hbm = pl.BlockSpec(memory_space=pltpu.HBM)
    vmem = pl.BlockSpec(memory_space=pltpu.VMEM)
    outs = pl.pallas_call(
        finish_kernel,
        out_shape=(
            *[jax.ShapeDtypeStruct(a_shape, F32)] * 3,
            *[jax.ShapeDtypeStruct(e_shape, F32)] * 3,
            jax.ShapeDtypeStruct((256, width), BF16),
            jax.ShapeDtypeStruct((16, 8, width), BF16),
        ),
        in_specs=[vmem] * 10,
        out_specs=(hbm,) * 8,
        scratch_shapes=[
            pltpu.VMEM((steps, 256, SUB), BF16),
            pltpu.VMEM((3,) + a_shape, F32),
            pltpu.VMEM((3,) + e_shape, F32),
            pltpu.VMEM((256, 256), BF16),
            pltpu.SemaphoreType.DMA((2 * steps + 6,)),
        ],
        compiler_params=pltpu.CompilerParams(vmem_limit_bytes=16 * 1024 * 1024),
    )(full_a.reshape(steps, 16, 2, 8, SUB), full_e.reshape(steps // 2, 16, 8, PART), g, f, *[v.reshape(a_shape) for v in attn_state], *exp_state)
    attn_new = [v.reshape(1, width) for v in outs[:3]]
    exp_new = [
        v.reshape(2 * ROWS, 2, LANES).transpose(1, 0, 2).reshape(1, 2, width) for v in outs[3:6]
    ]
    return (*attn_new, *exp_new, outs[6], outs[7].reshape(1, 128, width))


def solution(mesh):
    rows = P(("expert", "dp"), None)
    owned = P("expert", "dp", None)
    return jax.shard_map(
        body,
        mesh=mesh,
        in_specs=(rows, rows, owned, owned, rows, rows, rows, owned, owned, owned),
        out_specs=(rows, rows, rows, owned, owned, owned, P(), P("expert", None, None)),
        check_vma=False,
    )
```

```python
import math

import jax
import jax.numpy as jnp
from jax import lax
from jax.experimental import pallas as pl
from jax.experimental.pallas import tpu as pltpu
from jax.sharding import PartitionSpec as P

beta_first = 0.9
beta_second = 0.95
bias_first = 1.0 - 0.9**10
bias_second = 1.0 - 0.95**10
learn_rate = 0.01
decay_rate = 0.1
adam_eps = 1e-08

MESH = pl.DeviceIdType.MESH
F32 = jnp.float32
BF16 = jnp.bfloat16
HALF = 3072
PART = 1536
LANES = 128
ROWS = HALF // LANES
PROWS = PART // LANES
SUB = 768
SROWS = SUB // LANES


def adamw(grad, weight, moment, second, factor):
    scaled = factor * grad
    moment_new = beta_first * moment + (1.0 - beta_first) * scaled
    second_new = beta_second * second + (1.0 - beta_second) * scaled * scaled
    update = moment_new / bias_first / (jnp.sqrt(second_new / bias_second) + adam_eps)
    weight_new = weight - learn_rate * (update + decay_rate * weight)
    return (weight_new, moment_new, second_new)


def grouped(row):
    low = row & 3
    x = (row >> 2) & 3
    y = (row >> 4) & 3
    z_lo = row >> 6
    return ((y * 4 + x) * 4 + z_lo) * 4 + low


def device_at(z, y, x, core):
    return (z & 3, y * 16 + x * 4 + (z >> 2) * 2 + core)


def aligned(index, multiple):
    return pl.multiple_of(index, multiple)


def comm_kernel(
    limit,
    act_a_hbm, dy_a_hbm, act_e_hbm, dy_e_hbm, w_a_hbm, m_a_hbm, v_a_hbm, w_e_hbm, m_e_hbm, v_e_hbm,
    g_out, f_out, full_a, full_e,
    act_a, dy_a, act_e, dy_e, w_e, m_e, v_e,
    lhs_a, lhs_e, st_a, st_e, pf_a, pf_e,
    cs, cr, own, s1, r1, own2, s2, r2,
    s3_a, s3_e, z3_a, z3_e, r3_a, r3_e,
    n_s, n_r,
    ws_a, ws_e, gr_a, gr_e, g3_a, g3_e,
    send_sem, recv_sem, local_sem,
):
    z_lo = lax.axis_index("expert")
    dp = lax.axis_index("dp")
    core = dp & 1
    z_hi = (dp >> 1) & 1
    x = (dp >> 2) & 3
    y = dp >> 4
    z = z_hi * 4 + z_lo
    other = 1 - core
    peer = device_at(z, y, x, other)

    zc_places, zc_devices, plane_devices = {}, {}, {}
    for dz in range(8):
        for dc in range(2):
            oz, oc = (z + dz) & 7, core if dc == 0 else other
            zc_places[dz, dc] = (oz, oc)
            zc_devices[dz, dc] = device_at(oz, y, x, oc)
    for dy in range(4):
        for dx in range(4):
            plane_devices[dy, dx] = device_at(z, (y + dy) & 3, (x + dx) & 3, core)

    def plane_mate(dy, dx):
        return plane_devices[dy, dx]

    def axis_mate(axis, d):
        return plane_mate(d, 0) if axis == 0 else plane_mate(0, d)

    place = (y, x)

    kept = []
    waited = []

    def keep(src, dst):
        copy = pltpu.make_async_copy(src, dst, local_sem.at[len(kept)])
        copy.start()
        kept.append(copy)
        return copy

    def need(copies):
        for copy in copies:
            copy.wait()
            waited.append(copy)

    sent = []
    arrived = []

    def send(src, dst, where):
        i = len(sent)
        copy = pltpu.make_async_remote_copy(
            src_ref=src, dst_ref=dst, send_sem=send_sem.at[i], recv_sem=recv_sem.at[i],
            device_id=where, device_id_type=MESH,
        )
        copy.start()
        sent.append(copy)
        return copy

    def arrive(copies):
        for copy in copies:
            copy.wait_recv()
            arrived.append(copy)

    def finish_all():
        arrive([copy for copy in sent if not any(copy is done for done in arrived)])
        for copy in [copy for copy in kept if not any(copy is done for done in waited)]:
            copy.wait()
        for copy in sent:
            copy.wait_send()

    need_act = (keep(act_a_hbm, act_a), keep(act_e_hbm.at[0], act_e))
    barrier = pltpu.get_barrier_semaphore()
    greeted = 0
    for dz in range(8):
        for dc in range(2):
            if dz or dc:
                oz, oc = zc_places[dz, dc]
                pl.semaphore_signal(barrier, inc=1, device_id=zc_devices[dz, dc], device_id_type=MESH)
                greeted += 1
    for dy in range(4):
        for dx in range(4):
            if dy or dx:
                pl.semaphore_signal(barrier, inc=1, device_id=plane_mate(dy, dx), device_id_type=MESH)
                greeted += 1

    need_dy = {}
    for half in range(2):
        for s in range(4):
            cols = pl.ds(aligned((other if half == 0 else core) * HALF + s * SUB, SUB), SUB)
            need_dy[half, s] = (
                keep(dy_a_hbm.at[:, cols], dy_a.at[:, cols]),
                keep(dy_e_hbm.at[0, :, cols], dy_e.at[:, cols]),
            )
    need_state = [
        keep(src, st_a.at[:, pl.ds(k * ROWS, ROWS)]) for k, src in enumerate((w_a_hbm, m_a_hbm, v_a_hbm))
    ] + [keep(src, dst) for src, dst in ((w_e_hbm, w_e), (m_e_hbm, m_e), (v_e_hbm, v_e))]

    r0 = lax.broadcasted_iota(jnp.int32, (256, 256), 0)
    r1_ = lax.broadcasted_iota(jnp.int32, (256, 256), 1)
    pick = jnp.where(r0 == grouped(r1_), 1.0, 0.0).astype(BF16)
    need(need_act)
    lhs_a[...] = lax.dot_general(
        pick, act_a[...], (((1,), (1,)), ((), ())), preferred_element_type=F32
    ).astype(BF16)
    e0 = lax.broadcasted_iota(jnp.int32, (128, 128), 0)
    e1 = lax.broadcasted_iota(jnp.int32, (128, 128), 1)
    same = jnp.where(e0 == e1, 1.0, 0.0).astype(BF16)
    lhs_e[...] = lax.dot_general(
        same, act_e[...], (((1,), (1,)), ((), ())), preferred_element_type=F32
    ).astype(BF16)

    def terms(half, s):
        need(need_dy[half, s])
        cols = pl.ds(aligned((other if half == 0 else core) * HALF + s * SUB, SUB), SUB)
        ga = jnp.dot(lhs_a[...], dy_a[:, cols], preferred_element_type=F32)
        ge = jnp.dot(lhs_e[...], dy_e[:, cols], preferred_element_type=F32)
        return ga.reshape(4, 4, 2, 8, SUB), ge.reshape(4, 4, 8, SUB)

    def piece(ref, part, second, first):
        return ref.at[part, second, first] if part % 2 == 0 else ref.at[part, first, second]

    order = (2, 1, 3, 0)
    copies_c, copies_1 = {}, {}

    def give(s):
        ga, ge = terms(0, s)
        cs[s, :, :, 0:2] = ga.astype(BF16)
        cs[s, :, :, 2] = ge.astype(BF16)
        if s == 0:
            pl.semaphore_wait(barrier, greeted)
        copies_c[s] = send(cs.at[s], cr.at[s], peer)

    def take(s):
        ga, ge = terms(1, s)
        own[s, :, :, 0:2] = ga
        own[s, :, :, 2] = ge
        arrive([copies_c[s]])
        for b in range(4):
            both = own[s, b] + cr[s, b].astype(F32)
            own[s, b] = both
            s1[s, b] = both.astype(BF16)
        first = 1 - s % 2
        if s < 3:
            copies_1[s] = []
            for e in (2, 1, 3):
                to = ((place[first] + e) & 3)
                src = s1.at[s, :, to] if s % 2 == 0 else s1.at[s, to]
                copies_1[s].append(send(src, r1.at[s, e - 1], axis_mate(first, e)))
        else:
            for d in order:
                at = ((place[s % 2] + d) & 3)
                copies_1[s, d] = [
                    send(
                        piece(s1, s, at, ((place[first] + e) & 3)),
                        r1.at[s, e - 1, at],
                        axis_mate(first, e),
                    )
                    for e in (2, 1, 3)
                ]

    give(0)
    z_order = (4, 3, 5, 2, 6, 1, 7, 0)
    my_q = z_lo * 4 + z_hi * 2 + core
    my_e = z_hi * 2 + core
    need(need_state)
    for h in range(2):
        for j in range(2):
            for k, state in enumerate((w_e, m_e, v_e)):
                st_e[h, pl.ds((j * 3 + k) * ROWS, ROWS), :] = state[pl.ds(h * 2 * ROWS + j, ROWS, stride=2), :]
    pf_at_a = pl.ds(aligned(my_q * 3 * ROWS, 8), 3 * ROWS)
    pf_at_e = pl.ds(aligned(my_e * 6 * ROWS, 8), 6 * ROWS)
    copies_pf = []
    for dz in z_order:
        for dc in range(2):
            if dz or dc:
                oz, oc = zc_places[dz, dc]
                copies_pf.append(send(st_a.at[oc], pf_a.at[pf_at_a], zc_devices[dz, dc]))
                if dz in (0, 4):
                    copies_pf.append(send(st_e.at[oc], pf_e.at[pf_at_e], zc_devices[dz, dc]))
    pf_a[pf_at_a, :] = st_a[core]
    pf_e[pf_at_e, :] = st_e[core]

    give(1)
    take(0)
    take(1)
    give(2)
    give(3)
    take(2)
    take(3)

    copies_2 = {s: [] for s in range(4)}

    def pass_on(s, d):
        at = ((place[s % 2] + d) & 3)
        total = piece(own, s, at, place[1 - s % 2])[...]
        for e in range(3):
            total = total + r1[s, e, at].astype(F32)
        if d:
            s2[s, d - 1] = total.astype(BF16)
            copies_2[s].append(send(s2.at[s, d - 1], r2.at[s, d - 1], axis_mate(s % 2, d)))
        else:
            own2[s] = total

    for s in (0, 1, 2):
        arrive(copies_1[s])
        for d in order:
            pass_on(s, d)
    for d in order:
        for s in (3,):
            arrive(copies_1[s, d])
            pass_on(s, d)

    for s in range(4):
        arrive(copies_2[s])
        total = own2[s]
        for d in range(3):
            total = total + r2[s, d].astype(F32)
        total_a = total[0:2].reshape(16, SUB)
        total_e = total[2]
        for t in range(SROWS):
            lanes = slice(t * LANES, (t + 1) * LANES)
            s3_a[pl.ds(s * SROWS + t, 16, stride=ROWS), :] = total_a[:, lanes]
            s3_e[pl.ds(s * SROWS + t, 8, stride=ROWS), :] = total_e[:, lanes]
    z3_a[...] = s3_a[...].astype(BF16).reshape(16, ROWS, LANES)
    z3_e[...] = s3_e[...].astype(BF16).reshape(4, 2 * ROWS, LANES)

    batch = []
    for dz in z_order:
        for dc in range(2):
            if dz or dc:
                oz, oc = zc_places[dz, dc]
                q = (oz & 3) * 4 + (oz >> 2) * 2 + oc
                batch.append(send(z3_a.at[q], r3_a.at[dc, dz], zc_devices[dz, dc]))
                if dz in (0, 4):
                    q = (oz >> 2) * 2 + oc
                    batch.append(send(z3_e.at[q], r3_e.at[dc, dz // 4], zc_devices[dz, dc]))
    arrive(batch)

    near = s3_a[pl.ds(aligned(my_q * ROWS, 8), ROWS), :]
    far = r3_a[1, 0].astype(F32)
    for dz in range(1, 8):
        near = near + r3_a[0, dz].astype(F32)
        far = far + r3_a[1, dz].astype(F32)
    near_at = pl.ds(aligned(core * ROWS, 8), ROWS)
    far_at = pl.ds(aligned(other * ROWS, 8), ROWS)
    g_out[0, near_at, :] = near
    g_out[0, far_at, :] = far
    near_e = s3_e[pl.ds(aligned(my_e * 2 * ROWS, 8), 2 * ROWS), :] + r3_e[0, 1].astype(F32)
    far_e = r3_e[1, 0].astype(F32) + r3_e[1, 1].astype(F32)
    for j in range(2):
        g_out[1 + j, near_at, :] = near_e[j * ROWS : (j + 1) * ROWS]
        g_out[1 + j, far_at, :] = far_e[j * ROWS : (j + 1) * ROWS]

    square = jnp.zeros((8, LANES), F32)
    for piece in (near, far, near_e, far_e):
        for i in range(piece.shape[0] // 8):
            part_of = piece[i * 8 : (i + 1) * 8]
            square = square + part_of * part_of
    n_s[0] = square
    batch = []
    for dz in z_order:
        for dc in range(2):
            if dz or dc:
                oz, oc = zc_places[dz, dc]
                batch.append(send(n_s.at[0], n_r.at[0, dz * 2 + dc], zc_devices[dz, dc]))
    ws_a[core] = near.astype(BF16)
    ws_a[other] = far.astype(BF16)
    ws_e[core] = near_e.astype(BF16)
    ws_e[other] = far_e.astype(BF16)
    copies_g = []
    for dz in z_order:
        for dc in range(2):
            if dz or dc:
                oz, oc = zc_places[dz, dc]
                copies_g.append(send(ws_a.at[oc], gr_a.at[my_q], zc_devices[dz, dc]))
                if dz in (0, 4):
                    copies_g.append(send(ws_e.at[oc], gr_e.at[my_e], zc_devices[dz, dc]))
    gr_a[my_q] = ws_a[core]
    gr_e[my_e] = ws_e[core]
    arrive(batch)
    for i in range(1, 16):
        square = square + n_r[0, i]
    n_s[1] = square
    batch = []
    for dy in order:
        for dx in order:
            if dy or dx:
                batch.append(send(n_s.at[1], n_r.at[1, dy * 4 + dx], plane_mate(dy, dx)))
    arrive(copies_g)
    g3_a[...] = gr_a[...].astype(F32).reshape(16 * ROWS, LANES)
    g3_e[...] = gr_e[...].astype(F32).reshape(8 * ROWS, LANES)
    arrive(copies_pf)
    arrive(batch)
    for i in range(1, 16):
        square = square + n_r[1, i]
    norm = jnp.sqrt(jnp.sum(square, keepdims=True))
    factor = jnp.minimum(1.0, limit / (norm + 1e-06))
    f_out[...] = jnp.broadcast_to(factor, (8, LANES))

    def new_tile(rows, grad, state, t):
        values = [state[pl.ds(k * ROWS + t, rows, stride=3 * ROWS), :] for k in range(3)]
        return adamw(grad[pl.ds(t, rows, stride=ROWS), :], *values, factor)[0].astype(BF16)

    even = ((z_lo + 1) & 2)
    odd = (z_lo & 2) + 1
    mine = (even, odd)
    swapped = (2 - even, 4 - odd)
    swap_z = (z + 1 - 2 * (z & 1), (z + 7 + 2 * (z & 1)) & 7)

    def spread(ref, lead, part, at):
        here = block(ref, lead, part, at, place[1 - part])
        return [send(here, here, axis_mate(1 - part, e)) for e in (2, 1, 3)]

    def block(ref, lead, part, second, first):
        return ref.at[lead, second, first] if part == 0 else ref.at[lead, first, second]

    def strip(ref, lead, part, second):
        return ref.at[lead, second] if part == 0 else ref.at[lead, :, second]

    def deliver(ref, lead, part, second):
        src = strip(ref, lead, part, second)
        send(src, src, peer)

    gt_a = full_a.at[core]
    gt_e = full_e.at[core]
    first_a, second_a, first_e, second_e = {}, {}, {}, {}
    for part in range(2):
        for t in range(SROWS):
            tile = new_tile(16, g3_a, pf_a, mine[part] * SROWS + t)
            gt_a[mine[part], y, x, :, :, pl.ds(t * LANES, LANES)] = tile.reshape(2, 8, LANES)
        here = gt_a.at[mine[part], y, x]
        for d in (2, 1, 3):
            second_a[part, d] = send(here, here, axis_mate(part, d))
        first_a[part, 0] = spread(gt_a, mine[part], part, place[part])
    for part in range(2):
        for t in range(PROWS):
            gt_e[part, y, x, :, pl.ds(t * LANES, LANES)] = new_tile(8, g3_e, pf_e, part * PROWS + t)
        here = gt_e.at[part, y, x]
        for d in (2, 1, 3):
            second_e[part, d] = send(here, here, axis_mate(part, d))

    def from_mate(part, d):
        return ((place[part] + 4 - d) & 3)

    for d in (1, 3, 2):
        for part in range(2):
            arrive([second_a[part, d]])
            first_a[part, d] = spread(gt_a, mine[part], part, from_mate(part, d))
    for part in range(2):
        arrive([second_e[part, d] for d in (1, 3, 2)])
        for e in (2, 1, 3):
            here = gt_e.at[0, :, x] if part == 0 else gt_e.at[1, y]
            first_e[part, e] = send(here, here, axis_mate(1 - part, e))
    swaps = {}

    def pass_attention(d):
        for part in range(2):
            at = from_mate(part, d)
            arrive(first_a[part, d])
            ready = strip(gt_a, mine[part], part, at)
            swaps[part, d] = send(ready, ready, device_at(swap_z[part], y, x, core))
            deliver(gt_a, mine[part], part, at)

    def end_expert(e):
        for part in range(2):
            if e:
                arrive([first_e[part, e]])
            at = (place[1 - part] + 4 - e) & 3
            src = gt_e.at[0, :, at] if part == 0 else gt_e.at[1, at]
            send(src, src, peer)

    def end_swap(d):
        for part in range(2):
            arrive([swaps[part, d]])
            deliver(gt_a, swapped[part], part, from_mate(part, d))

    pass_attention(0)
    pass_attention(1)
    end_expert(0)
    pass_attention(3)
    end_swap(0)
    pass_attention(2)
    end_expert(1)
    end_swap(1)
    end_expert(3)
    end_swap(3)
    end_expert(2)
    end_swap(2)
    finish_all()


def finish_kernel(
    full_a, full_e, g, f, w_a, m_a, v_a, w_e, m_e, v_e,
    wa_o, ma_o, va_o, we_o, me_o, ve_o, attn_o, exp_o,
    attn, new_a, new_e, pick, out_sem,
):
    r0 = lax.broadcasted_iota(jnp.int32, (256, 256), 0)
    r1 = lax.broadcasted_iota(jnp.int32, (256, 256), 1)
    pick[...] = jnp.where(grouped(r0) == r1, 1.0, 0.0).astype(BF16)

    writes = []

    def write(src, dst):
        copy = pltpu.make_async_copy(src, dst, out_sem.at[len(writes)])
        copy.start()
        writes.append(copy)

    for i in range(2 * HALF // PART):
        write(full_e.at[i], exp_o.at[:, :, pl.ds(i * PART, PART)])
    for i in range(2 * HALF // SUB):
        gathered = full_a[i].reshape(256, SUB)
        attn[i] = jnp.dot(pick[...], gathered, preferred_element_type=F32).astype(BF16)
        write(attn.at[i], attn_o.at[:, pl.ds(i * SUB, SUB)])
    factor = f[0:1, 0:1]
    new = adamw(g[0], w_a[...], m_a[...], v_a[...], factor)
    for k, ref in enumerate((wa_o, ma_o, va_o)):
        new_a[k] = new[k]
        write(new_a.at[k], ref)
    for j in range(2):
        rows = pl.ds(j, 2 * ROWS, stride=2)
        new = adamw(g[1 + j], w_e[rows, :], m_e[rows, :], v_e[rows, :], factor)
        for k in range(3):
            new_e[k, rows, :] = new[k]
    for k, ref in enumerate((we_o, me_o, ve_o)):
        write(new_e.at[k], ref)
    for copy in writes:
        copy.wait()


def comm_part(act_attn, dy_attn, act_exp, dy_exp, w_attn, m_attn, v_attn, w_exp, m_exp, v_exp):
    width = w_attn.shape[1]
    total_params = width * (act_attn.shape[1] + lax.axis_size("expert") * act_exp.shape[2])
    limit = 0.5 * math.sqrt(total_params)
    attn_state = [v.reshape(2, ROWS, LANES) for v in (w_attn, m_attn, v_attn)]
    exp_state = [
        v.reshape(2, 2 * ROWS, LANES).transpose(1, 0, 2).reshape(4 * ROWS, LANES)
        for v in (w_exp, m_exp, v_exp)
    ]
    hbm = pl.BlockSpec(memory_space=pltpu.HBM)
    vmem = pl.BlockSpec(memory_space=pltpu.VMEM)
    n_send = 230

    def blocks(dtype, *lead):
        return pltpu.VMEM(lead + (3, 8, SUB), dtype)

    outs = pl.pallas_call(
        lambda *refs: comm_kernel(limit, *refs),
        out_shape=(
            jax.ShapeDtypeStruct((3, 2 * ROWS, LANES), F32),
            jax.ShapeDtypeStruct((8, LANES), F32),
            jax.ShapeDtypeStruct((2, 4, 4, 4, 2, 8, SUB), BF16),
            jax.ShapeDtypeStruct((2, 2, 4, 4, 8, PART), BF16),
        ),
        in_specs=[hbm] * 10,
        out_specs=(vmem,) * 4,
        scratch_shapes=[
            pltpu.VMEM((256, 256), BF16),
            pltpu.VMEM((256, 4 * PART), BF16),
            pltpu.VMEM((128, 128), BF16),
            pltpu.VMEM((128, 4 * PART), BF16),
            *[pltpu.VMEM((4 * ROWS, LANES), F32)] * 3,
            pltpu.VMEM((256, 256), BF16),
            pltpu.VMEM((128, 128), BF16),
            pltpu.VMEM((2, 3 * ROWS, LANES), F32),
            pltpu.VMEM((2, 6 * ROWS, LANES), F32),
            pltpu.VMEM((16 * 3 * ROWS, LANES), F32),
            pltpu.VMEM((8 * 3 * ROWS, LANES), F32),
            blocks(BF16, 4, 4, 4),
            blocks(BF16, 4, 4, 4),
            blocks(F32, 4, 4, 4),
            blocks(BF16, 4, 4, 4),
            blocks(BF16, 4, 3, 4),
            blocks(F32, 4),
            blocks(BF16, 4, 3),
            blocks(BF16, 4, 3),
            pltpu.VMEM((16 * ROWS, LANES), F32),
            pltpu.VMEM((8 * ROWS, LANES), F32),
            pltpu.VMEM((16, ROWS, LANES), BF16),
            pltpu.VMEM((4, 2 * ROWS, LANES), BF16),
            pltpu.VMEM((2, 8, ROWS, LANES), BF16),
            pltpu.VMEM((2, 2, 2 * ROWS, LANES), BF16),
            pltpu.VMEM((2, 8, LANES), F32),
            pltpu.VMEM((2, 16, 8, LANES), F32),
            pltpu.VMEM((2, ROWS, LANES), BF16),
            pltpu.VMEM((2, 2 * ROWS, LANES), BF16),
            pltpu.VMEM((16, ROWS, LANES), BF16),
            pltpu.VMEM((4, 2 * ROWS, LANES), BF16),
            pltpu.VMEM((16 * ROWS, LANES), F32),
            pltpu.VMEM((8 * ROWS, LANES), F32),
            pltpu.SemaphoreType.DMA((n_send,)),
            pltpu.SemaphoreType.DMA((n_send,)),
            pltpu.SemaphoreType.DMA((80,)),
        ],
        compiler_params=pltpu.CompilerParams(
            collective_id=0, has_side_effects=True, vmem_limit_bytes=36 * 1024 * 1024
        ),
    )(*[pltpu.with_memory_space_constraint(v, pltpu.HBM) for v in (act_attn, dy_attn, act_exp, dy_exp, *attn_state, *exp_state)])
    return outs, attn_state, exp_state


def body(act_attn, dy_attn, act_exp, dy_exp, *state):
    width = dy_attn.shape[1]
    (g, f, full_a, full_e), attn_state, exp_state = comm_part(act_attn, dy_attn, act_exp, dy_exp, *state)
    a_shape, e_shape = (2 * ROWS, LANES), (4 * ROWS, LANES)
    steps = width // SUB
    hbm = pl.BlockSpec(memory_space=pltpu.HBM)
    vmem = pl.BlockSpec(memory_space=pltpu.VMEM)
    outs = pl.pallas_call(
        finish_kernel,
        out_shape=(
            *[jax.ShapeDtypeStruct(a_shape, F32)] * 3,
            *[jax.ShapeDtypeStruct(e_shape, F32)] * 3,
            jax.ShapeDtypeStruct((256, width), BF16),
            jax.ShapeDtypeStruct((16, 8, width), BF16),
        ),
        in_specs=[vmem] * 10,
        out_specs=(hbm,) * 8,
        scratch_shapes=[
            pltpu.VMEM((steps, 256, SUB), BF16),
            pltpu.VMEM((3,) + a_shape, F32),
            pltpu.VMEM((3,) + e_shape, F32),
            pltpu.VMEM((256, 256), BF16),
            pltpu.SemaphoreType.DMA((2 * steps + 6,)),
        ],
        compiler_params=pltpu.CompilerParams(vmem_limit_bytes=16 * 1024 * 1024),
    )(full_a.reshape(steps, 16, 2, 8, SUB), full_e.reshape(steps // 2, 16, 8, PART), g, f, *[v.reshape(a_shape) for v in attn_state], *exp_state)
    attn_new = [v.reshape(1, width) for v in outs[:3]]
    exp_new = [
        v.reshape(2 * ROWS, 2, LANES).transpose(1, 0, 2).reshape(1, 2, width) for v in outs[3:6]
    ]
    return (*attn_new, *exp_new, outs[6], outs[7].reshape(1, 128, width))


def solution(mesh):
    rows = P(("expert", "dp"), None)
    owned = P("expert", "dp", None)
    return jax.shard_map(
        body,
        mesh=mesh,
        in_specs=(rows, rows, owned, owned, rows, rows, rows, owned, owned, owned),
        out_specs=(rows, rows, rows, owned, owned, owned, P(), P("expert", None, None)),
        check_vma=False,
    )
```
